768 devices in a mesh: space: 64 (over x, y, core), chan: 12 (over z).
Axes of the slice: x: 4, y: 8, z: 12, core: 2. Of those that a mesh axis runs over, the one named last changes fastest.
Arguments:
- field: bfloat16 [288, 6144, 32], P('chan', 'space'), may hold values from -6 to 6
- grad_out: bfloat16 [288, 6144, 32], P('chan', 'space'), may hold values from -6 to 6
- filters: bfloat16 [9, 288, 288], replicated, may hold values from -0.125 to 0.125
Outputs:
- grad_field: float32 [288, 6144, 32], P('chan', 'space')
- grad_filters: float32 [9, 288, 288], P(None, 'chan')
The draws below stay inside these ranges and needn't reach their ends.
All inputs are finite; a program needn't handle non-finite values.
Results may differ from the reference program's by a relative error of at most 0.0003.
Values may be sent and summed in bfloat16 or wider, within the bound.
No kernel may reach another device: no remote copies, remote signals or barrier semaphores. Data moves between devices by JAX's collectives and lax.ppermute only.
A program may use at most 64 MiB of HBM per device.

```python
import math
import jax
import jax.numpy as jnp
from jax import lax

CH = 288
COL_DEV = 96
COLS = 6144
ROWS = 32


def block_scale(key, dims, cuts, smallest, largest):
    def one(axis_at, blocks):
        draws = jax.random.uniform(jax.random.fold_in(jax.random.fold_in(key, 6), axis_at), (blocks,), jnp.float32, smallest / len(cuts), largest / len(cuts))
        return jnp.repeat(jnp.exp(draws), dims[axis_at] // blocks).reshape((-1,) + (1,) * (len(dims) - axis_at - 1))

    level = one(*cuts[0])
    for cut in cuts[1:]:
        level = level * one(*cut)
    return level


def centred(stream_key, shape, spread, bound, shards=(), kind=jnp.bfloat16):
    values = spread * jax.random.normal(stream_key, shape, jnp.float32)
    if shards:
        values = values * block_scale(stream_key, shape, shards, -0.22, 0.18)
    return jnp.clip(values, -bound, bound).astype(kind)


def setup_inputs(seed: int = 0) -> dict:
    arg_keys = jax.random.split(jax.random.key(seed), 4)
    field = centred(arg_keys[0], (CH, COLS, ROWS), 1.0, 6.0, ((0, 12), (1, 64)))
    grad_out = centred(arg_keys[1], (CH, COLS, ROWS), 1.0, 6.0, ((0, 12), (1, 64)))
    filters = centred(arg_keys[2], (9, CH, CH), (9 * CH) ** -0.5, 0.125)
    return {"field": field, "grad_out": grad_out, "filters": filters}


def reference(field, grad_out, filters):
    chans, cols_all, rows = field.shape
    padded = jnp.pad(grad_out, ((0, 0), (2, 2), (2, 2)))
    weights = filters.astype(jnp.float32)
    blocks = cols_all // COL_DEV

    def step(acc, index):
        begin = (index * COL_DEV).astype(jnp.int32)
        x_blk = lax.dynamic_slice_in_dim(field, begin, COL_DEV, 1).astype(jnp.float32)
        g_blk = lax.dynamic_slice_in_dim(padded, begin, COL_DEV + 4, 1).astype(jnp.float32)
        result = jnp.zeros((chans, COL_DEV, rows), jnp.float32)
        parts = []
        for a in range(3):
            for b in range(3):
                k = a * 3 + b
                shifted = g_blk[:, 4 - 2 * a:4 - 2 * a + COL_DEV, 4 - 2 * b:4 - 2 * b + rows]
                result = result + jnp.einsum('io,owr->iwr', weights[k], shifted, precision=lax.Precision.HIGHEST)
                parts.append(jnp.einsum('iwr,owr->io', x_blk, shifted, precision=lax.Precision.HIGHEST))
        return (acc + jnp.stack(parts), result)
    total, pieces = lax.scan(step, jnp.zeros((9, chans, chans), jnp.float32), jnp.arange(blocks, dtype=jnp.int32))
    grad_field = jnp.transpose(pieces, (1, 0, 2, 3)).reshape(chans, cols_all, rows)
    return (grad_field, total * (1.0 / math.sqrt(rows * cols_all)))
```

```python
import math

import jax
import jax.numpy as jnp
from jax import lax
from jax.sharding import PartitionSpec as P

NX, NY, NCORE = 4, 8, 2


def group_lists():
    def at(x, y, core):
        return (x * NY + y) * NCORE + core

    across = [[at(x, y, c) for x in range(NX) for c in range(NCORE)] for y in range(NY)]
    along = [[at(x, y, c) for y in range(NY)] for x in range(NX) for c in range(NCORE)]
    return across, along


def per_device(field, grad_out, filters):
    across, along = group_lists()
    spaces = lax.axis_size("space")
    chans = lax.axis_size("chan")
    chan_dev, width, rows = field.shape
    factor = 1.0 / math.sqrt(rows * width * spaces)
    layer = lax.axis_index("chan")

    def move(cells, step):
        return lax.ppermute(cells, "chan", [(i, (i + step) % chans) for i in range(chans)])

    def spread(piece, groups):
        stacked = jnp.broadcast_to(piece[None], (8,) + piece.shape)
        return lax.all_to_all(stacked, "space", 0, 0, axis_index_groups=groups, tiled=True)

    source = field.transpose(0, 2, 1)
    cells = grad_out.transpose(0, 2, 1)
    left = lax.ppermute(cells[:, :, -2:], "space", [(i, i + 1) for i in range(spaces - 1)])
    right = lax.ppermute(cells[:, :, :2], "space", [(i + 1, i) for i in range(spaces - 1)])
    sources = [move(source, 1), source, move(source, -1), move(source, -2)]
    bordered = jnp.concatenate([left, cells, right], axis=2)
    grads = jnp.stack([move(bordered, 4), bordered, move(bordered, -4)])
    third = layer // 4
    grads = jnp.concatenate(
        [lax.dynamic_index_in_dim(grads, (m - third + 4) % 3, 0, False) for m in range(3)]
    )
    padded = jnp.pad(grads, ((0, 0), (2, 2), (0, 0)))
    window = jnp.concatenate(sources)

    first, last = filters[:, : 2 * chan_dev], filters[:, -chan_dev:]
    own = jnp.concatenate([last, filters, first], axis=1)
    own = lax.dynamic_slice_in_dim(own, layer * chan_dev, 4 * chan_dev, 1)
    lane = jnp.arange(3 * chan_dev)
    wanted = (4 * (lane // chan_dev) + layer % 4) * chan_dev + lane % chan_dev
    chosen = (jnp.arange(12 * chan_dev)[:, None] == wanted[None, :]).astype(filters.dtype)
    own = jnp.einsum("kio,op->kip", own, chosen, preferred_element_type=jnp.float32)
    own = own.astype(filters.dtype).reshape(3, 3, 4 * chan_dev, 3 * chan_dev)

    parts = []
    result = jnp.zeros((4 * chan_dev, rows, width), jnp.float32)
    for b in range(3):
        row = []
        for a in range(3):
            shifted = padded[:, 4 - 2 * b : 4 - 2 * b + rows, 4 - 2 * a : 4 - 2 * a + width]
            row.append(
                jnp.einsum("irw,orw->io", window, shifted, preferred_element_type=jnp.float32)
            )
            result = result + jnp.einsum(
                "io,orw->irw", own[a, b], shifted, preferred_element_type=jnp.float32
            )
        parts.append(jnp.pad(jnp.concatenate(row, axis=1), ((0, 0), (0, 40))))
    parts = jnp.stack(parts).reshape(3, 4, chan_dev, 2, 128)
    parts = parts.transpose(1, 3, 0, 2, 4).reshape(8, 3 * chan_dev, 128)

    piece = lax.all_to_all(parts, "space", 0, 0, axis_index_groups=across, tiled=True).sum(0)
    home = [
        (s * chans + c, s * chans + (c - 1 + s // (NY * NCORE)) % chans)
        for s in range(spaces)
        for c in range(chans)
    ]
    piece = lax.ppermute(piece, ("space", "chan"), home)
    piece = spread(piece, along).sum(0)
    whole = spread(piece, across).reshape(4, 2, 3, chan_dev, 128)
    whole = whole.transpose(0, 2, 3, 1, 4).reshape(4, 3, chan_dev, 256)[..., :216]
    whole = whole.reshape(4, 3, chan_dev, 3, 3, chan_dev)
    whole = jnp.stack(
        [lax.dynamic_index_in_dim(whole, (layer + 1 - v + 4) % 4, 0, False) for v in range(4)]
    )
    whole = whole.transpose(3, 1, 2, 4, 0, 5)
    grad_filters = whole.reshape(9, chan_dev, 12 * chan_dev) * factor

    blocks = result.reshape(4, chan_dev, rows, width)
    total = blocks[1] + move(blocks[0], -1) + move(blocks[2], 1) + move(blocks[3], 2)
    return (total.transpose(0, 2, 1), grad_filters)


def solution(mesh):
    in_specs = (P("chan", "space", None), P("chan", "space", None), P())
    out_specs = (P("chan", "space", None), P(None, "chan", None))
    return jax.shard_map(
        per_device, mesh=mesh, in_specs=in_specs, out_specs=out_specs, check_vma=False
    )
```

```python
import functools
import math

import jax
import jax.numpy as jnp
from jax import lax
from jax.experimental import pallas as pl
from jax.experimental.pallas import tpu as pltpu
from jax.sharding import PartitionSpec as P

NX, NY, NCORE = 4, 8, 2
LANES = 128
VMEM = pl.BlockSpec(memory_space=pltpu.VMEM)
SMEM = pl.BlockSpec(memory_space=pltpu.SMEM)


def group_lists():
    def at(x, y, core):
        return (x * NY + y) * NCORE + core

    across = [[at(x, y, c) for x in range(NX) for c in range(NCORE)] for y in range(NY)]
    along = [[at(x, y, c) for y in range(NY)] for x in range(NX) for c in range(NCORE)]
    return across, along


def lane_index(chans):
    return lax.broadcasted_iota(jnp.int32, (chans, LANES), 1)


def edges_kernel(cells_ref, edges_ref):
    rows, chans, width = cells_ref.shape[0], cells_ref.shape[1], 96
    lane = lane_index(chans)
    packed = jnp.zeros((chans, LANES), jnp.float32)
    for r in range(rows):
        row = cells_ref[r].astype(jnp.float32)
        tail = pltpu.roll(row, (2 * r - (width - 2)) % LANES, 1)
        head = pltpu.roll(row, (2 * rows + 2 * r) % LANES, 1)
        packed = jnp.where((lane >= 2 * r) & (lane < 2 * r + 2), tail, packed)
        at = 2 * rows + 2 * r
        packed = jnp.where((lane >= at) & (lane < at + 2), head, packed)
    edges_ref[...] = packed.astype(edges_ref.dtype)


def border_kernel(cells_ref, left_ref, right_ref, out_ref):
    rows, chans, width = cells_ref.shape[0], cells_ref.shape[1], 96
    lane = lane_index(chans)
    left = left_ref[...].astype(jnp.float32)
    right = right_ref[...].astype(jnp.float32)
    for r in range(rows):
        row = pltpu.roll(cells_ref[r].astype(jnp.float32), 2, 1)
        row = jnp.where(lane < 2, pltpu.roll(left, (-2 * r) % LANES, 1), row)
        at = width + 2
        tail = pltpu.roll(right, (at - 2 * rows - 2 * r) % LANES, 1)
        row = jnp.where((lane >= at) & (lane < at + 2), tail, row)
        out_ref[r] = row.astype(out_ref.dtype)


def weights_kernel(third_ref, x0, x1, x2, x3, g0, g1, g2, parts_ref, shifted_ref, window_ref):
    rows, chans = x0.shape[0], x0.shape[1]
    third = third_ref[0]
    blank = jnp.zeros((9 * chans, 2 * LANES), shifted_ref.dtype)
    shifted_ref[:, : 2 * LANES] = blank
    shifted_ref[:, (rows + 2) * LANES :] = blank
    for r in range(rows):
        window = jnp.concatenate([x[r].astype(jnp.float32) for x in (x0, x1, x2, x3)], axis=0)
        window_ref[:, r * LANES : (r + 1) * LANES] = window.astype(window_ref.dtype)
        near, own, far = [g[r].astype(jnp.float32) for g in (g0, g1, g2)]
        orders = ((own, far, near), (near, own, far), (far, near, own))
        base = jnp.concatenate(
            [
                jnp.where(third == 0, a, jnp.where(third == 1, b, c))
                for a, b, c in zip(*orders)
            ],
            axis=0,
        )
        taps = [pltpu.roll(base, LANES - 4, 1), pltpu.roll(base, LANES - 2, 1), base]
        shifted_ref[:, (r + 2) * LANES : (r + 3) * LANES] = jnp.concatenate(taps, axis=0).astype(
            shifted_ref.dtype
        )
    for b in range(3):
        at = (4 - 2 * b) * LANES
        part = lax.dot_general(
            window_ref[...],
            shifted_ref[:, at : at + rows * LANES],
            (((1,), (1,)), ((), ())),
            preferred_element_type=jnp.float32,
        )
        part = jnp.concatenate([part, jnp.zeros((4 * chans, 5 * 8), jnp.float32)], axis=1)
        for j in range(4):
            for h in range(2):
                parts_ref[2 * j + h, b * chans : (b + 1) * chans] = part[
                    j * chans : (j + 1) * chans, h * LANES : (h + 1) * LANES
                ]


def inputs_kernel(shifted_ref, filters_ref, *out_refs):
    rows, chans = out_refs[0].shape[0], out_refs[0].shape[1]
    total = None
    for b in range(3):
        at = (4 - 2 * b) * LANES
        part = jnp.dot(
            filters_ref[b],
            shifted_ref[:, at : at + rows * LANES],
            preferred_element_type=jnp.float32,
        )
        total = part if total is None else total + part
    for j in range(4):
        for r in range(rows):
            out_refs[j][r] = total[
                j * chans : (j + 1) * chans, r * LANES : (r + 1) * LANES
            ]


def place_kernel(factor, layer_ref, whole_ref, out_ref):
    chans = out_ref.shape[1]
    layer = layer_ref[0]
    for b in range(3):
        rows = []
        for v in range(4):
            j = lax.rem(layer + 5 - v, 4)
            rows.append(
                jnp.concatenate(
                    [whole_ref[2 * j + h, b * chans : (b + 1) * chans] for h in range(2)], axis=1
                )
            )
        for a in range(3):
            pieces = []
            for m in range(3):
                at = (3 * a + m) * chans
                pieces += [rows[v][:, at : at + chans] for v in range(4)]
            out_ref[3 * a + b] = jnp.concatenate(pieces, axis=1) * factor


def call(kernel, outs, ins, scalars=0, scratch=()):
    return pl.pallas_call(
        kernel,
        out_shape=outs,
        in_specs=[SMEM] * scalars + [VMEM] * (ins - scalars),
        out_specs=jax.tree.map(lambda _: VMEM, outs),
        scratch_shapes=list(scratch),
        compiler_params=pltpu.CompilerParams(vmem_limit_bytes=40 << 20),
    )


def per_device(field, grad_out, filters):
    across, along = group_lists()
    spaces = lax.axis_size("space")
    chans = lax.axis_size("chan")
    chan_dev, width, rows = field.shape
    factor = 1.0 / math.sqrt(rows * width * spaces)
    layer = lax.axis_index("chan")
    kind, wide = field.dtype, jnp.float32

    def shape(*dims, dtype=kind):
        return jax.ShapeDtypeStruct(dims, dtype)

    def move(cells, step):
        return lax.ppermute(cells, "chan", [(i, (i + step) % chans) for i in range(chans)])

    def spread(piece, groups):
        stacked = jnp.broadcast_to(piece[None], (8,) + piece.shape)
        return lax.all_to_all(stacked, "space", 0, 0, axis_index_groups=groups, tiled=True)

    def by_row(cells):
        return jnp.pad(cells.transpose(2, 0, 1), ((0, 0), (0, 0), (0, LANES - width)))

    cells = by_row(grad_out)
    edges = call(edges_kernel, shape(chan_dev, LANES), 1)(cells)
    left = lax.ppermute(edges, "space", [(i, i + 1) for i in range(spaces - 1)])
    right = lax.ppermute(edges, "space", [(i + 1, i) for i in range(spaces - 1)])
    edges, field = lax.optimization_barrier((edges, field))
    source = by_row(field)
    sources = [move(source, 1), source, move(source, -1), move(source, -2)]
    bordered = call(border_kernel, shape(rows, chan_dev, LANES), 3)(cells, left, right)
    grads = [move(bordered, 4), bordered, move(bordered, -4)]

    first, last = filters[:, : 2 * chan_dev], filters[:, -chan_dev:]
    own = jnp.concatenate([last, filters, first], axis=1)
    own = lax.dynamic_slice_in_dim(own, layer * chan_dev, 4 * chan_dev, 1)
    lane = jnp.arange(3 * chan_dev)
    wanted = (4 * (lane // chan_dev) + layer % 4) * chan_dev + lane % chan_dev
    chosen = (jnp.arange(12 * chan_dev)[:, None] == wanted[None, :]).astype(filters.dtype)
    own = jnp.einsum("kio,op->kip", own, chosen, preferred_element_type=jnp.float32)
    own = own.astype(filters.dtype).reshape(3, 3, 4 * chan_dev, 3 * chan_dev)
    own = own.transpose(1, 2, 0, 3).reshape(3, 4 * chan_dev, 9 * chan_dev)

    third = (layer // 4)[None]
    parts, shifted = call(
        weights_kernel,
        (
            shape(8, 3 * chan_dev, LANES, dtype=wide),
            shape(9 * chan_dev, (rows + 4) * LANES),
        ),
        8,
        1,
        [pltpu.VMEM((4 * chan_dev, rows * LANES), kind)],
    )(third, *sources, *grads)

    piece = lax.all_to_all(parts, "space", 0, 0, axis_index_groups=across, tiled=True).sum(0)
    home = [
        (s * chans + c, s * chans + (c - 1 + s // (NY * NCORE)) % chans)
        for s in range(spaces)
        for c in range(chans)
    ]
    piece = lax.ppermute(piece, ("space", "chan"), home)
    piece = spread(piece, along).sum(0)
    whole = spread(piece, across)
    grad_filters = call(
        functools.partial(place_kernel, factor),
        shape(9, chan_dev, 12 * chan_dev, dtype=wide),
        2,
        1,
    )(layer[None], whole)

    blocks = call(
        inputs_kernel, tuple(shape(rows, chan_dev, LANES, dtype=wide) for _ in range(4)), 2
    )(shifted, own)
    total = blocks[1] + move(blocks[0], -1) + move(blocks[2], 1) + move(blocks[3], 2)
    return (total[..., :width].transpose(1, 2, 0), grad_filters)


def solution(mesh):
    in_specs = (P("chan", "space", None), P("chan", "space", None), P())
    out_specs = (P("chan", "space", None), P(None, "chan", None))
    return jax.shard_map(
        per_device, mesh=mesh, in_specs=in_specs, out_specs=out_specs, check_vma=False
    )
```

```python
import functools
import math

import jax
import jax.numpy as jnp
from jax import lax
from jax.experimental import pallas as pl
from jax.experimental.pallas import tpu as pltpu
from jax.sharding import PartitionSpec as P

NX, NY, NCORE = 4, 8, 2
LANES, WIDTH = 128, 96
VMEM = pl.BlockSpec(memory_space=pltpu.VMEM)
SMEM = pl.BlockSpec(memory_space=pltpu.SMEM)


def group_lists():
    def at(x, y, core):
        return (x * NY + y) * NCORE + core

    across = [[at(x, y, c) for x in range(NX) for c in range(NCORE)] for y in range(NY)]
    along = [[at(x, y, c) for y in range(NY)] for x in range(NX) for c in range(NCORE)]
    return across, along


def lane_index(chans):
    return lax.broadcasted_iota(jnp.int32, (chans, LANES), 1)


def edges_kernel(cells_ref, edges_ref, dense_ref):
    rows, chans = cells_ref.shape[0], cells_ref.shape[1]
    lane = lane_index(chans)
    packed = jnp.zeros((chans, LANES), jnp.float32)
    for start in range(0, rows, 4):
        group = [cells_ref[start + i].astype(jnp.float32) for i in range(4)]
        store_dense(dense_ref, start, group)
        for i in range(4):
            r = start + i
            tail_at, head_at = 4 * r, (4 * r + WIDTH + 2) % LANES
            tail = pltpu.roll(group[i], (tail_at - (WIDTH - 2)) % LANES, 1)
            head = pltpu.roll(group[i], head_at, 1)
            packed = jnp.where((lane >= tail_at) & (lane < tail_at + 2), tail, packed)
            packed = jnp.where((lane >= head_at) & (lane < head_at + 2), head, packed)
    edges_ref[...] = packed.astype(edges_ref.dtype)


def store_dense(dense_ref, start, group):
    lane = lane_index(group[0].shape[0])
    turned = [group[0]] + [pltpu.roll(group[i], LANES - 32 * i, 1) for i in (1, 2, 3)]
    tiles = [jnp.where(lane < LANES - 32 * (i + 1), turned[i], turned[i + 1]) for i in range(3)]
    for i in range(3):
        at = (3 * start // 4 + i) * LANES
        dense_ref[:, at : at + LANES] = tiles[i].astype(dense_ref.dtype)


def load_rows(tiles, offset):
    lane = lane_index(tiles[0].shape[0])
    rows = []
    for i in range(4):
        turn = (32 * i + offset) % LANES
        row = pltpu.roll(tiles[min(i, 2)], turn, 1) if turn else tiles[i]
        if i in (1, 2):
            before = pltpu.roll(tiles[i - 1], turn, 1)
            row = jnp.where(lane < 32 * i + offset, before, row)
        rows.append(row)
    return rows


def border_kernel(dense_ref, left_ref, right_ref, source_ref, out_ref, packed_ref):
    for start in range(0, source_ref.shape[0], 4):
        group = [source_ref[start + i].astype(jnp.float32) for i in range(4)]
        store_dense(packed_ref, start, group)
    cells = dense_ref.shape[1]
    packed_ref[:, cells:] = jnp.zeros((dense_ref.shape[0], LANES), packed_ref.dtype)
    lane = lane_index(dense_ref.shape[0])
    left = left_ref[...].astype(jnp.float32)
    right = right_ref[...].astype(jnp.float32)
    out_ref[:, :cells] = dense_ref[...]
    out_ref[:, cells:] = jnp.where(lane % 4 < 2, left, right).astype(out_ref.dtype)


def weights_kernel(third_ref, own_ref, *refs):
    g_refs, x_refs, (parts_ref, shifted_ref, window_ref) = refs[:3], refs[3:7], refs[7:]
    chans = x_refs[0].shape[0]
    rows = refs[8].shape[1] // LANES - 4
    third = third_ref[0]
    kind = shifted_ref.dtype
    blank = jnp.zeros((9 * chans, 2 * LANES), kind)
    shifted_ref[:, : 2 * LANES] = blank
    shifted_ref[:, (rows + 2) * LANES :] = blank
    lane_x, lane_g = lane_index(4 * chans), lane_index(3 * chans)

    def pick(at):
        near, own, far = [g[:, at : at + LANES].astype(jnp.float32) for g in g_refs]
        orders = ((own, far, near), (near, own, far), (far, near, own))
        return jnp.concatenate(
            [
                jnp.where(third == 0, a, jnp.where(third == 1, b, c))
                for a, b, c in zip(*orders)
            ],
            axis=0,
        )

    sides = pick(rows * WIDTH)
    for start in range(0, rows, 4):
        ats = [(3 * start // 4 + i) * LANES for i in range(3)]
        tiles = [
            jnp.concatenate([x[:, at : at + LANES].astype(jnp.float32) for x in x_refs], axis=0)
            for at in ats
        ]
        for i, row in enumerate(load_rows(tiles, 0)):
            at = (start + i) * LANES
            window_ref[:, at : at + LANES] = jnp.where(lane_x < WIDTH, row, 0.0).astype(kind)
        for i, row in enumerate(load_rows([pick(at) for at in ats], 2)):
            side = pltpu.roll(sides, (-4 * (start + i)) % LANES, 1) if start + i else sides
            row = jnp.where((lane_g >= 2) & (lane_g < WIDTH + 2), row, side)
            row = jnp.where(lane_g < WIDTH + 4, row, 0.0)
            taps = [pltpu.roll(row, LANES - 4, 1), pltpu.roll(row, LANES - 2, 1), row]
            at = (start + i + 2) * LANES
            shifted_ref[:, at : at + LANES] = jnp.concatenate(taps, axis=0).astype(kind)
    for b in range(3):
        at = (4 - 2 * b) * LANES
        part = lax.dot_general(
            window_ref[...],
            shifted_ref[:, at : at + rows * LANES],
            (((1,), (1,)), ((), ())),
            preferred_element_type=jnp.float32,
        )
        part = jnp.concatenate([part, jnp.zeros((4 * chans, 5 * 8), jnp.float32)], axis=1)
        for j in range(4):
            for h in range(2):
                parts_ref[2 * j + h, b * chans : (b + 1) * chans] = part[
                    j * chans : (j + 1) * chans, h * LANES : (h + 1) * LANES
                ]


def inputs_kernel(shifted_ref, filters_ref, *out_refs):
    chans = out_refs[0].shape[0]
    rows = out_refs[0].shape[1] // WIDTH
    total = None
    for b in range(3):
        at = (4 - 2 * b) * LANES
        part = jnp.dot(
            filters_ref[b],
            shifted_ref[:, at : at + rows * LANES],
            preferred_element_type=jnp.float32,
        )
        total = part if total is None else total + part
    for j in range(4):
        block = total[j * chans : (j + 1) * chans]
        for start in range(0, rows, 4):
            group = [block[:, r * LANES : (r + 1) * LANES] for r in range(start, start + 4)]
            store_dense(out_refs[j], start, group)


def total_kernel(a_ref, b_ref, c_ref, d_ref, out_ref):
    for start in range(0, out_ref.shape[1], 4):
        tiles = []
        for i in range(3):
            at = pl.ds((3 * start // 4 + i) * LANES, LANES)
            tiles.append((a_ref[:, at] + b_ref[:, at]) + (c_ref[:, at] + d_ref[:, at]))
        for i, row in enumerate(load_rows(tiles, 0)):
            out_ref[:, start + i, :] = row[:, :WIDTH]


def copies_kernel(in_ref, out_ref):
    piece = in_ref[0]
    for i in range(1, in_ref.shape[0]):
        piece = piece + in_ref[i]
    for i in range(out_ref.shape[0]):
        out_ref[i] = piece


def place_kernel(factor, layer_ref, whole_ref, out_ref):
    chans = out_ref.shape[1]
    layer = layer_ref[0]
    for b in range(3):
        rows = []
        for v in range(4):
            j = lax.rem(layer + 5 - v, 4)
            rows.append(
                jnp.concatenate(
                    [whole_ref[2 * j + h, b * chans : (b + 1) * chans] for h in range(2)], axis=1
                )
            )
        for a in range(3):
            pieces = []
            for m in range(3):
                at = (3 * a + m) * chans
                pieces += [rows[v][:, at : at + chans] for v in range(4)]
            out_ref[3 * a + b] = jnp.concatenate(pieces, axis=1) * factor


def call(kernel, outs, ins, scalars=0, scratch=()):
    return pl.pallas_call(
        kernel,
        out_shape=outs,
        in_specs=[SMEM] * scalars + [VMEM] * (ins - scalars),
        out_specs=jax.tree.map(lambda _: VMEM, outs),
        scratch_shapes=list(scratch),
        compiler_params=pltpu.CompilerParams(vmem_limit_bytes=40 << 20),
    )


def per_device(field, grad_out, filters):
    across, along = group_lists()
    spaces = lax.axis_size("space")
    chans = lax.axis_size("chan")
    chan_dev, width, rows = field.shape
    factor = 1.0 / math.sqrt(rows * width * spaces)
    layer = lax.axis_index("chan")
    kind, wide = field.dtype, jnp.float32

    def shape(*dims, dtype=kind):
        return jax.ShapeDtypeStruct(dims, dtype)

    def move(cells, step):
        return lax.ppermute(cells, "chan", [(i, (i + step) % chans) for i in range(chans)])

    def exchange(parts, groups):
        return lax.all_to_all(parts, "space", 0, 0, axis_index_groups=groups, tiled=True)

    def added(parts, copies):
        return call(copies_kernel, shape(copies, *parts.shape[1:], dtype=wide), 1)(parts)

    def by_row(cells):
        return jnp.pad(cells.transpose(2, 0, 1), ((0, 0), (0, 0), (0, LANES - width)))

    cells = rows * width
    edges, dense = call(edges_kernel, (shape(chan_dev, LANES), shape(chan_dev, cells)), 1)(
        by_row(grad_out)
    )
    left = lax.ppermute(edges, "space", [(i, i + 1) for i in range(spaces - 1)])
    right = lax.ppermute(edges, "space", [(i + 1, i) for i in range(spaces - 1)])
    edges, field = lax.optimization_barrier((edges, field))
    bordered, source = call(
        border_kernel, (shape(chan_dev, cells + LANES), shape(chan_dev, cells + LANES)), 4
    )(dense, left, right, by_row(field))
    grads = [move(bordered, 4), bordered, move(bordered, -4)]
    sources = [move(source, 1), source, move(source, -1), move(source, -2)]

    first, last = filters[:, : 2 * chan_dev], filters[:, -chan_dev:]
    own = jnp.concatenate([last, filters, first], axis=1)
    own = lax.dynamic_slice_in_dim(own, layer * chan_dev, 4 * chan_dev, 1)
    lane = jnp.arange(3 * chan_dev)
    wanted = (4 * (lane // chan_dev) + layer % 4) * chan_dev + lane % chan_dev
    chosen = (jnp.arange(12 * chan_dev)[:, None] == wanted[None, :]).astype(filters.dtype)
    own = jnp.einsum("kio,op->kip", own, chosen, preferred_element_type=jnp.float32)
    own = own.astype(filters.dtype).reshape(3, 3, 4 * chan_dev, 3 * chan_dev)
    own = own.transpose(1, 2, 0, 3).reshape(3, 4 * chan_dev, 9 * chan_dev)

    third = (layer // 4)[None]
    parts, shifted = call(
        weights_kernel,
        (
            shape(8, 3 * chan_dev, LANES, dtype=wide),
            shape(9 * chan_dev, (rows + 4) * LANES),
        ),
        9,
        1,
        [pltpu.VMEM((4 * chan_dev, rows * LANES), kind)],
    )(third, own, *grads, *sources)
    blocks = call(
        inputs_kernel, tuple(shape(chan_dev, cells, dtype=wide) for _ in range(4)), 2
    )(shifted, own)

    piece = added(exchange(parts, across), 1)
    piece, *blocks = lax.optimization_barrier((piece, *blocks))
    home = [
        (s * chans + c, s * chans + (c - 1 + s // (NY * NCORE)) % chans)
        for s in range(spaces)
        for c in range(chans)
    ]
    piece = lax.ppermute(piece, ("space", "chan"), home)
    others = [move(blocks[0], -1), move(blocks[2], 1), move(blocks[3], 2)]
    piece = added(exchange(added(piece, 8), along), 8)
    whole = exchange(piece, across)
    grad_filters = call(
        functools.partial(place_kernel, factor),
        shape(9, chan_dev, 12 * chan_dev, dtype=wide),
        2,
        1,
    )(layer[None], whole)
    total = call(total_kernel, shape(chan_dev, rows, width, dtype=wide), 4)(blocks[1], *others)
    return (total.transpose(0, 2, 1), grad_filters)


def solution(mesh):
    in_specs = (P("chan", "space", None), P("chan", "space", None), P())
    out_specs = (P("chan", "space", None), P(None, "chan", None))
    return jax.shard_map(
        per_device, mesh=mesh, in_specs=in_specs, out_specs=out_specs, check_vma=False
    )
```

```python
import functools
import math

import jax
import jax.numpy as jnp
from jax import lax
from jax.experimental import pallas as pl
from jax.experimental.pallas import tpu as pltpu
from jax.sharding import PartitionSpec as P

NX, NY, NCORE = 4, 8, 2
LANES, WIDTH = 128, 96
VMEM = pl.BlockSpec(memory_space=pltpu.VMEM)
SMEM = pl.BlockSpec(memory_space=pltpu.SMEM)


def group_lists():
    def at(x, y, core):
        return (x * NY + y) * NCORE + core

    across = [[at(x, y, c) for x in range(NX) for c in range(NCORE)] for y in range(NY)]
    along = [[at(x, y, c) for y in range(NY)] for x in range(NX) for c in range(NCORE)]
    return across, along


def lane_index(chans):
    return lax.broadcasted_iota(jnp.int32, (chans, LANES), 1)


def pack_kernel(cells_ref, dense_ref):
    for start in range(0, cells_ref.shape[0], 4):
        store_dense(dense_ref, start, [cells_ref[start + i].astype(jnp.float32) for i in range(4)])


def edges_kernel(near_ref, own_ref, far_ref, edges_ref):
    refs = (near_ref, own_ref, far_ref)
    rows = near_ref.shape[1] // WIDTH
    lane = lane_index(3 * near_ref.shape[0])
    packed = jnp.zeros(edges_ref.shape, jnp.float32)
    for r in range(rows):
        for column, to in ((WIDTH - 2, 4 * r), (0, (4 * r + WIDTH + 2) % LANES)):
            tile, at = divmod(r * WIDTH + column, LANES)
            cut = slice(tile * LANES, (tile + 1) * LANES)
            block = jnp.concatenate([ref[:, cut].astype(jnp.float32) for ref in refs], axis=0)
            turn = (to - at) % LANES
            block = pltpu.roll(block, turn, 1) if turn else block
            packed = jnp.where((lane >= to) & (lane < to + 2), block, packed)
    edges_ref[...] = packed.astype(edges_ref.dtype)


def store_dense(dense_ref, start, group):
    lane = lane_index(group[0].shape[0])
    turned = [group[0]] + [pltpu.roll(group[i], LANES - 32 * i, 1) for i in (1, 2, 3)]
    tiles = [jnp.where(lane < LANES - 32 * (i + 1), turned[i], turned[i + 1]) for i in range(3)]
    for i in range(3):
        at = (3 * start // 4 + i) * LANES
        dense_ref[:, at : at + LANES] = tiles[i].astype(dense_ref.dtype)


def load_rows(tiles, offset):
    lane = lane_index(tiles[0].shape[0])
    rows = []
    for i in range(4):
        turn = (32 * i + offset) % LANES
        row = pltpu.roll(tiles[min(i, 2)], turn, 1) if turn else tiles[i]
        if i in (1, 2):
            before = pltpu.roll(tiles[i - 1], turn, 1)
            row = jnp.where(lane < 32 * i + offset, before, row)
        rows.append(row)
    return rows


def shift_kernel(third_ref, near_ref, own_ref, far_ref, left_ref, right_ref, shifted_ref):
    refs = (near_ref, own_ref, far_ref)
    chans = near_ref.shape[0]
    rows = near_ref.shape[1] // WIDTH
    third = third_ref[0]
    kind = shifted_ref.dtype
    blank = jnp.zeros((9 * chans, 2 * LANES), kind)
    shifted_ref[:, : 2 * LANES] = blank
    shifted_ref[:, (rows + 2) * LANES :] = blank
    lane = lane_index(3 * chans)

    def ordered(near, own, far):
        orders = ((own, far, near), (near, own, far), (far, near, own))
        return jnp.concatenate(
            [
                jnp.where(third == 0, a, jnp.where(third == 1, b, c))
                for a, b, c in zip(*orders)
            ],
            axis=0,
        )

    sides = jnp.where(
        lane % 4 < 2, left_ref[...].astype(jnp.float32), right_ref[...].astype(jnp.float32)
    )
    sides = ordered(*[sides[m * chans : (m + 1) * chans] for m in range(3)])
    for start in range(0, rows, 4):
        ats = [(3 * start // 4 + i) * LANES for i in range(3)]
        tiles = [
            ordered(*[ref[:, at : at + LANES].astype(jnp.float32) for ref in refs]) for at in ats
        ]
        for i, row in enumerate(load_rows(tiles, 2)):
            side = pltpu.roll(sides, (-4 * (start + i)) % LANES, 1) if start + i else sides
            row = jnp.where((lane >= 2) & (lane < WIDTH + 2), row, side)
            row = jnp.where(lane < WIDTH + 4, row, 0.0)
            taps = [pltpu.roll(row, LANES - 4, 1), pltpu.roll(row, LANES - 2, 1), row]
            at = (start + i + 2) * LANES
            shifted_ref[:, at : at + LANES] = jnp.concatenate(taps, axis=0).astype(kind)


def weights_kernel(own_ref, x0, x1, x2, x3, shifted_ref, parts_ref, window_ref):
    refs = (x0, x1, x2, x3)
    chans = x0.shape[0]
    rows = x0.shape[1] // WIDTH
    lane = lane_index(4 * chans)
    for start in range(0, rows, 4):
        ats = [(3 * start // 4 + i) * LANES for i in range(3)]
        tiles = [
            jnp.concatenate([x[:, at : at + LANES].astype(jnp.float32) for x in refs], axis=0)
            for at in ats
        ]
        for i, row in enumerate(load_rows(tiles, 0)):
            at = (start + i) * LANES
            row = jnp.where(lane < WIDTH, row, 0.0)
            window_ref[:, at : at + LANES] = row.astype(window_ref.dtype)
    for b in range(3):
        at = (4 - 2 * b) * LANES
        part = lax.dot_general(
            window_ref[...],
            shifted_ref[:, at : at + rows * LANES],
            (((1,), (1,)), ((), ())),
            preferred_element_type=jnp.float32,
        )
        part = jnp.concatenate([part, jnp.zeros((4 * chans, 5 * 8), jnp.float32)], axis=1)
        for j in range(4):
            for h in range(2):
                parts_ref[2 * j + h, b * chans : (b + 1) * chans] = part[
                    j * chans : (j + 1) * chans, h * LANES : (h + 1) * LANES
                ]


def inputs_kernel(shifted_ref, filters_ref, *out_refs):
    chans = out_refs[0].shape[0]
    rows = out_refs[0].shape[1] // WIDTH
    total = None
    for b in range(3):
        at = (4 - 2 * b) * LANES
        part = jnp.dot(
            filters_ref[b],
            shifted_ref[:, at : at + rows * LANES],
            preferred_element_type=jnp.float32,
        )
        total = part if total is None else total + part
    for j in range(4):
        block = total[j * chans : (j + 1) * chans]
        for start in range(0, rows, 4):
            group = [block[:, r * LANES : (r + 1) * LANES] for r in range(start, start + 4)]
            store_dense(out_refs[j], start, group)


def total_kernel(a_ref, b_ref, c_ref, d_ref, out_ref):
    for start in range(0, out_ref.shape[1], 4):
        tiles = []
        for i in range(3):
            at = pl.ds((3 * start // 4 + i) * LANES, LANES)
            tiles.append((a_ref[:, at] + b_ref[:, at]) + (c_ref[:, at] + d_ref[:, at]))
        for i, row in enumerate(load_rows(tiles, 0)):
            out_ref[:, start + i, :] = row[:, :WIDTH]


def copies_kernel(in_ref, out_ref):
    piece = in_ref[0]
    for i in range(1, in_ref.shape[0]):
        piece = piece + in_ref[i]
    for i in range(out_ref.shape[0]):
        out_ref[i] = piece


def place_kernel(factor, layer_ref, whole_ref, out_ref):
    chans = out_ref.shape[1]
    layer = layer_ref[0]
    for b in range(3):
        rows = []
        for v in range(4):
            j = lax.rem(layer + 5 - v, 4)
            rows.append(
                jnp.concatenate(
                    [whole_ref[2 * j + h, b * chans : (b + 1) * chans] for h in range(2)], axis=1
                )
            )
        for a in range(3):
            pieces = []
            for m in range(3):
                at = (3 * a + m) * chans
                pieces += [rows[v][:, at : at + chans] for v in range(4)]
            out_ref[3 * a + b] = jnp.concatenate(pieces, axis=1) * factor


def call(kernel, outs, ins, scalars=0, scratch=()):
    return pl.pallas_call(
        kernel,
        out_shape=outs,
        in_specs=[SMEM] * scalars + [VMEM] * (ins - scalars),
        out_specs=jax.tree.map(lambda _: VMEM, outs),
        scratch_shapes=list(scratch),
        compiler_params=pltpu.CompilerParams(vmem_limit_bytes=40 << 20),
    )


def per_device(field, grad_out, filters):
    across, along = group_lists()
    spaces = lax.axis_size("space")
    chans = lax.axis_size("chan")
    chan_dev, width, rows = field.shape
    factor = 1.0 / math.sqrt(rows * width * spaces)
    layer = lax.axis_index("chan")
    kind, wide = field.dtype, jnp.float32

    def shape(*dims, dtype=kind):
        return jax.ShapeDtypeStruct(dims, dtype)

    def move(cells, step):
        return lax.ppermute(cells, "chan", [(i, (i + step) % chans) for i in range(chans)])

    def exchange(parts, groups):
        return lax.all_to_all(parts, "space", 0, 0, axis_index_groups=groups, tiled=True)

    def added(parts, copies):
        return call(copies_kernel, shape(copies, *parts.shape[1:], dtype=wide), 1)(parts)

    def by_row(cells):
        return jnp.pad(cells.transpose(2, 0, 1), ((0, 0), (0, 0), (0, LANES - width)))

    cells = rows * width
    dense = call(pack_kernel, shape(chan_dev, cells), 1)(by_row(grad_out))
    grads = [move(dense, 4), dense, move(dense, -4)]
    source = call(pack_kernel, shape(chan_dev, cells), 1)(by_row(field))
    sources = [move(source, 1), source, move(source, -1), move(source, -2)]
    edges = call(edges_kernel, shape(3 * chan_dev, LANES), 3)(*grads)
    left = lax.ppermute(edges, "space", [(i, i + 1) for i in range(spaces - 1)])
    right = lax.ppermute(edges, "space", [(i + 1, i) for i in range(spaces - 1)])

    first, last = filters[:, : 2 * chan_dev], filters[:, -chan_dev:]
    own = jnp.concatenate([last, filters, first], axis=1)
    own = lax.dynamic_slice_in_dim(own, layer * chan_dev, 4 * chan_dev, 1)
    lane = jnp.arange(3 * chan_dev)
    wanted = (4 * (lane // chan_dev) + layer % 4) * chan_dev + lane % chan_dev
    chosen = (jnp.arange(12 * chan_dev)[:, None] == wanted[None, :]).astype(filters.dtype)
    own = jnp.einsum("kio,op->kip", own, chosen, preferred_element_type=jnp.float32)
    own = own.astype(filters.dtype).reshape(3, 3, 4 * chan_dev, 3 * chan_dev)
    own = own.transpose(1, 2, 0, 3).reshape(3, 4 * chan_dev, 9 * chan_dev)

    third = (layer // 4)[None]
    shifted = call(shift_kernel, shape(9 * chan_dev, (rows + 4) * LANES), 6, 1)(
        third, *grads, left, right
    )
    parts = call(
        weights_kernel,
        shape(8, 3 * chan_dev, LANES, dtype=wide),
        6,
        0,
        [pltpu.VMEM((4 * chan_dev, rows * LANES), kind)],
    )(own, *sources, shifted)
    blocks = call(
        inputs_kernel, tuple(shape(chan_dev, cells, dtype=wide) for _ in range(4)), 2
    )(shifted, own)

    piece = added(exchange(parts, across), 1)
    piece, *blocks = lax.optimization_barrier((piece, *blocks))
    home = [
        (s * chans + c, s * chans + (c - 1 + s // (NY * NCORE)) % chans)
        for s in range(spaces)
        for c in range(chans)
    ]
    piece = lax.ppermute(piece, ("space", "chan"), home)
    others = [move(blocks[0], -1), move(blocks[2], 1), move(blocks[3], 2)]
    piece = added(exchange(added(piece, 8), along), 8)
    whole = exchange(piece, across)
    grad_filters = call(
        functools.partial(place_kernel, factor),
        shape(9, chan_dev, 12 * chan_dev, dtype=wide),
        2,
        1,
    )(layer[None], whole)
    total = call(total_kernel, shape(chan_dev, rows, width, dtype=wide), 4)(blocks[1], *others)
    return (total.transpose(0, 2, 1), grad_filters)


def solution(mesh):
    in_specs = (P("chan", "space", None), P("chan", "space", None), P())
    out_specs = (P("chan", "space", None), P(None, "chan", None))
    return jax.shard_map(
        per_device, mesh=mesh, in_specs=in_specs, out_specs=out_specs, check_vma=False
    )
```

```python
import functools
import math

import jax
import jax.numpy as jnp
from jax import lax
from jax.experimental import pallas as pl
from jax.experimental.pallas import tpu as pltpu
from jax.sharding import PartitionSpec as P

NX, NY, NCORE = 4, 8, 2
LANES, WIDTH = 128, 96
PLACE_FLOPS = 10**9
VMEM = pl.BlockSpec(memory_space=pltpu.VMEM)
SMEM = pl.BlockSpec(memory_space=pltpu.SMEM)


def group_lists():
    def at(x, y, core):
        return (x * NY + y) * NCORE + core

    across = [[at(x, y, c) for x in range(NX) for c in range(NCORE)] for y in range(NY)]
    along = [[at(x, y, c) for y in range(NY)] for x in range(NX) for c in range(NCORE)]
    return across, along


def lane_index(chans):
    return lax.broadcasted_iota(jnp.int32, (chans, LANES), 1)


def pack_kernel(grad_ref, field_ref, *dense_refs):
    for cells_ref, dense_ref in zip((grad_ref, field_ref), dense_refs):
        for start in range(0, cells_ref.shape[0], 4):
            group = [cells_ref[start + i].astype(jnp.float32) for i in range(4)]
            store_dense(dense_ref, start, group)


def edges_kernel(own_ref, near_ref, up_ref, down_ref, far_ref, edges_ref):
    refs = (near_ref, own_ref, far_ref)
    rows = near_ref.shape[1] // WIDTH
    lane = lane_index(3 * near_ref.shape[0])
    packed = jnp.zeros(edges_ref.shape, jnp.float32)
    for r in range(rows):
        for column, to in ((WIDTH - 2, 4 * r), (0, (4 * r + WIDTH + 2) % LANES)):
            tile, at = divmod(r * WIDTH + column, LANES)
            cut = slice(tile * LANES, (tile + 1) * LANES)
            block = jnp.concatenate([ref[:, cut].astype(jnp.float32) for ref in refs], axis=0)
            turn = (to - at) % LANES
            block = pltpu.roll(block, turn, 1) if turn else block
            packed = jnp.where((lane >= to) & (lane < to + 2), block, packed)
    edges_ref[...] = packed.astype(edges_ref.dtype)


def store_dense(dense_ref, start, group):
    lane = lane_index(group[0].shape[0])
    turned = [group[0]] + [pltpu.roll(group[i], LANES - 32 * i, 1) for i in (1, 2, 3)]
    tiles = [jnp.where(lane < LANES - 32 * (i + 1), turned[i], turned[i + 1]) for i in range(3)]
    for i in range(3):
        at = (3 * start // 4 + i) * LANES
        dense_ref[:, at : at + LANES] = tiles[i].astype(dense_ref.dtype)


def load_rows(tiles, offset):
    lane = lane_index(tiles[0].shape[0])
    rows = []
    for i in range(4):
        turn = (32 * i + offset) % LANES
        row = pltpu.roll(tiles[min(i, 2)], turn, 1) if turn else tiles[i]
        if i in (1, 2):
            before = pltpu.roll(tiles[i - 1], turn, 1)
            row = jnp.where(lane < 32 * i + offset, before, row)
        rows.append(row)
    return rows


def shift_kernel(third_ref, left_ref, right_ref, near_ref, own_ref, far_ref, shifted_ref):
    refs = (near_ref, own_ref, far_ref)
    chans = near_ref.shape[0]
    rows = near_ref.shape[1] // WIDTH
    third = third_ref[0]
    kind = shifted_ref.dtype
    blank = jnp.zeros((9 * chans, 2 * LANES), kind)
    shifted_ref[:, : 2 * LANES] = blank
    shifted_ref[:, (rows + 2) * LANES :] = blank
    lane = lane_index(3 * chans)

    def ordered(near, own, far):
        orders = ((own, far, near), (near, own, far), (far, near, own))
        return jnp.concatenate(
            [
                jnp.where(third == 0, a, jnp.where(third == 1, b, c))
                for a, b, c in zip(*orders)
            ],
            axis=0,
        )

    sides = jnp.where(
        lane % 4 < 2, left_ref[...].astype(jnp.float32), right_ref[...].astype(jnp.float32)
    )
    sides = ordered(*[sides[m * chans : (m + 1) * chans] for m in range(3)])
    for start in range(0, rows, 4):
        ats = [(3 * start // 4 + i) * LANES for i in range(3)]
        tiles = [
            ordered(*[ref[:, at : at + LANES].astype(jnp.float32) for ref in refs]) for at in ats
        ]
        for i, row in enumerate(load_rows(tiles, 2)):
            side = pltpu.roll(sides, (-4 * (start + i)) % LANES, 1) if start + i else sides
            row = jnp.where((lane >= 2) & (lane < WIDTH + 2), row, side)
            row = jnp.where(lane < WIDTH + 4, row, 0.0)
            taps = [pltpu.roll(row, LANES - 4, 1), pltpu.roll(row, LANES - 2, 1), row]
            at = (start + i + 2) * LANES
            shifted_ref[:, at : at + LANES] = jnp.concatenate(taps, axis=0).astype(kind)


def weights_kernel(own_ref, x0, x1, x2, x3, shifted_ref, parts_ref, window_ref):
    refs = (x0, x1, x2, x3)
    chans = x0.shape[0]
    rows = x0.shape[1] // WIDTH
    lane = lane_index(4 * chans)
    for start in range(0, rows, 4):
        ats = [(3 * start // 4 + i) * LANES for i in range(3)]
        tiles = [
            jnp.concatenate([x[:, at : at + LANES].astype(jnp.float32) for x in refs], axis=0)
            for at in ats
        ]
        for i, row in enumerate(load_rows(tiles, 0)):
            at = (start + i) * LANES
            row = jnp.where(lane < WIDTH, row, 0.0)
            window_ref[:, at : at + LANES] = row.astype(window_ref.dtype)
    for b in range(3):
        at = (4 - 2 * b) * LANES
        part = lax.dot_general(
            window_ref[...],
            shifted_ref[:, at : at + rows * LANES],
            (((1,), (1,)), ((), ())),
            preferred_element_type=jnp.float32,
        )
        part = jnp.concatenate([part, jnp.zeros((4 * chans, 5 * 8), jnp.float32)], axis=1)
        for j in range(4):
            for h in range(2):
                parts_ref[2 * j + h, b * chans : (b + 1) * chans] = part[
                    j * chans : (j + 1) * chans, h * LANES : (h + 1) * LANES
                ]


def inputs_kernel(shifted_ref, filters_ref, parts_ref, *out_refs):
    chans = out_refs[0].shape[0]
    rows = out_refs[0].shape[1] // WIDTH
    total = None
    for b in range(3):
        at = (4 - 2 * b) * LANES
        part = jnp.dot(
            filters_ref[b],
            shifted_ref[:, at : at + rows * LANES],
            preferred_element_type=jnp.float32,
        )
        total = part if total is None else total + part
    for j in range(4):
        block = total[j * chans : (j + 1) * chans]
        for start in range(0, rows, 4):
            group = [block[:, r * LANES : (r + 1) * LANES] for r in range(start, start + 4)]
            store_dense(out_refs[j], start, group)


def total_kernel(a_ref, b_ref, c_ref, d_ref, out_ref):
    for start in range(0, out_ref.shape[1], 4):
        tiles = []
        for i in range(3):
            at = pl.ds((3 * start // 4 + i) * LANES, LANES)
            tiles.append((a_ref[:, at] + b_ref[:, at]) + (c_ref[:, at] + d_ref[:, at]))
        for i, row in enumerate(load_rows(tiles, 0)):
            out_ref[:, start + i, :] = row[:, :WIDTH]


def copies_kernel(in_ref, out_ref):
    piece = in_ref[0]
    for i in range(1, in_ref.shape[0]):
        piece = piece + in_ref[i]
    for i in range(out_ref.shape[0]):
        out_ref[i] = piece


def place_kernel(factor, layer_ref, whole_ref, out_ref):
    chans = out_ref.shape[1]
    layer = layer_ref[0]
    for b in range(3):
        rows = []
        for v in range(4):
            j = lax.rem(layer + 5 - v, 4)
            rows.append(
                jnp.concatenate(
                    [whole_ref[2 * j + h, b * chans : (b + 1) * chans] for h in range(2)], axis=1
                )
            )
        for a in range(3):
            pieces = []
            for m in range(3):
                at = (3 * a + m) * chans
                pieces += [rows[v][:, at : at + chans] for v in range(4)]
            out_ref[3 * a + b] = jnp.concatenate(pieces, axis=1) * factor


def call(kernel, outs, ins, scalars=0, scratch=(), unread=0, cost=None):
    return pl.pallas_call(
        kernel,
        out_shape=outs,
        in_specs=[SMEM] * scalars
        + [VMEM] * (ins - scalars - unread)
        + [pl.BlockSpec(memory_space=pl.ANY)] * unread,
        out_specs=jax.tree.map(lambda _: VMEM, outs),
        scratch_shapes=list(scratch),
        compiler_params=pltpu.CompilerParams(vmem_limit_bytes=40 << 20),
        cost_estimate=cost,
    )


def per_device(field, grad_out, filters):
    across, along = group_lists()
    spaces = lax.axis_size("space")
    chans = lax.axis_size("chan")
    chan_dev, width, rows = field.shape
    factor = 1.0 / math.sqrt(rows * width * spaces)
    layer = lax.axis_index("chan")
    kind, wide = field.dtype, jnp.float32

    def shape(*dims, dtype=kind):
        return jax.ShapeDtypeStruct(dims, dtype)

    def move(cells, step):
        return lax.ppermute(cells, "chan", [(i, (i + step) % chans) for i in range(chans)])

    def exchange(parts, groups):
        return lax.all_to_all(parts, "space", 0, 0, axis_index_groups=groups, tiled=True)

    def added(parts, copies):
        return call(copies_kernel, shape(copies, *parts.shape[1:], dtype=wide), 1)(parts)

    def by_row(cells):
        return jnp.pad(cells.transpose(2, 0, 1), ((0, 0), (0, 0), (0, LANES - width)))

    cells = rows * width
    dense, source = call(pack_kernel, (shape(chan_dev, cells),) * 2, 2)(
        by_row(grad_out), by_row(field)
    )
    near, up, down, far = move(dense, 4), move(source, 1), move(source, -1), move(dense, -4)
    grads = [near, dense, far]
    sources = [up, source, down, move(source, -2)]
    edges = call(edges_kernel, shape(3 * chan_dev, LANES), 5)(
        dense, near, up, down, far
    )
    left = lax.ppermute(edges, "space", [(i, i + 1) for i in range(spaces - 1)])
    right = lax.ppermute(edges, "space", [(i + 1, i) for i in range(spaces - 1)])

    first, last = filters[:, : 2 * chan_dev], filters[:, -chan_dev:]
    own = jnp.concatenate([last, filters, first], axis=1)
    own = lax.dynamic_slice_in_dim(own, layer * chan_dev, 4 * chan_dev, 1)
    lane = jnp.arange(3 * chan_dev)
    wanted = (4 * (lane // chan_dev) + layer % 4) * chan_dev + lane % chan_dev
    chosen = (jnp.arange(12 * chan_dev)[:, None] == wanted[None, :]).astype(filters.dtype)
    own = jnp.einsum("kio,op->kip", own, chosen, preferred_element_type=jnp.float32)
    own = own.astype(filters.dtype).reshape(3, 3, 4 * chan_dev, 3 * chan_dev)
    own = own.transpose(1, 2, 0, 3).reshape(3, 4 * chan_dev, 9 * chan_dev)

    third = (layer // 4)[None]
    shifted = call(shift_kernel, shape(9 * chan_dev, (rows + 4) * LANES), 6, 1)(
        third, left, right, *grads
    )
    parts = call(
        weights_kernel,
        shape(8, 3 * chan_dev, LANES, dtype=wide),
        6,
        0,
        [pltpu.VMEM((4 * chan_dev, rows * LANES), kind)],
    )(own, *sources, shifted)
    blocks = call(
        inputs_kernel, tuple(shape(chan_dev, cells, dtype=wide) for _ in range(4)), 3, 0, (), 1
    )(shifted, own, parts)

    home = [
        (s * chans + c, s * chans + (c - 1 + s // (NY * NCORE)) % chans)
        for s in range(spaces)
        for c in range(chans)
    ]
    def gathered(arrived):
        piece = lax.ppermute(added(arrived, 1), ("space", "chan"), home)
        piece = added(exchange(added(piece, 8), along), 8)
        return exchange(piece, across)

    whole = lax.cond(layer >= 0, gathered, lambda arrived: arrived, exchange(parts, across))
    grad_filters = call(
        functools.partial(place_kernel, factor),
        shape(9, chan_dev, 12 * chan_dev, dtype=wide),
        2,
        1,
        cost=pl.CostEstimate(flops=PLACE_FLOPS, bytes_accessed=0, transcendentals=0),
    )(layer[None], whole)
    others = [move(blocks[0], -1), move(blocks[2], 1), move(blocks[3], 2)]
    total = call(total_kernel, shape(chan_dev, rows, width, dtype=wide), 4)(blocks[1], *others)
    return (total.transpose(0, 2, 1), grad_filters)


def solution(mesh):
    in_specs = (P("chan", "space", None), P("chan", "space", None), P())
    out_specs = (P("chan", "space", None), P(None, "chan", None))
    return jax.shard_map(
        per_device, mesh=mesh, in_specs=in_specs, out_specs=out_specs, check_vma=False
    )
```

```python
import functools
import math

import jax
import jax.numpy as jnp
from jax import lax
from jax.experimental import pallas as pl
from jax.experimental.pallas import tpu as pltpu
from jax.sharding import PartitionSpec as P

NX, NY, NCORE = 4, 8, 2
LANES, WIDTH = 128, 96
TAIL = WIDTH - 2
VMEM = pl.BlockSpec(memory_space=pltpu.VMEM)
SMEM = pl.BlockSpec(memory_space=pltpu.SMEM)


def group_lists():
    def at(x, y, core):
        return (x * NY + y) * NCORE + core

    across = [[at(x, y, c) for x in range(NX) for c in range(NCORE)] for y in range(NY)]
    along = [[at(x, y, c) for y in range(NY)] for x in range(NX) for c in range(NCORE)]
    return across, along


def lane_index(chans):
    return lax.broadcasted_iota(jnp.int32, (chans, LANES), 1)


def pack_kernel(cells_ref, dense_ref):
    for start in range(0, cells_ref.shape[0], 4):
        store_dense(dense_ref, start, [cells_ref[start + i].astype(jnp.float32) for i in range(4)])


def edges_kernel(near_ref, own_ref, far_ref, edges_ref):
    refs = (near_ref, own_ref, far_ref)
    rows = near_ref.shape[1] // WIDTH
    lane = lane_index(3 * near_ref.shape[0])
    packed = jnp.zeros(edges_ref.shape, jnp.float32)
    for r in range(rows):
        for column, to in ((TAIL, 4 * r), (0, (4 * r + TAIL) % LANES)):
            tile, at = divmod(r * WIDTH + column, LANES)
            cut = slice(tile * LANES, (tile + 1) * LANES)
            block = jnp.concatenate([ref[:, cut].astype(jnp.float32) for ref in refs], axis=0)
            turn = (to - at) % LANES
            block = pltpu.roll(block, turn, 1) if turn else block
            packed = jnp.where((lane >= to) & (lane < to + 2), block, packed)
    edges_ref[...] = packed.astype(edges_ref.dtype)


def store_dense(dense_ref, start, group):
    lane = lane_index(group[0].shape[0])
    turned = [group[0]] + [pltpu.roll(group[i], LANES - 32 * i, 1) for i in (1, 2, 3)]
    tiles = [jnp.where(lane < LANES - 32 * (i + 1), turned[i], turned[i + 1]) for i in range(3)]
    for i in range(3):
        at = (3 * start // 4 + i) * LANES
        dense_ref[:, at : at + LANES] = tiles[i].astype(dense_ref.dtype)


def load_rows(tiles, offset):
    lane = lane_index(tiles[0].shape[0])
    rows = []
    for i in range(4):
        turn = (32 * i + offset) % LANES
        row = pltpu.roll(tiles[min(i, 2)], turn, 1) if turn else tiles[i]
        if i in (1, 2):
            before = pltpu.roll(tiles[i - 1], turn, 1)
            row = jnp.where(lane < 32 * i + offset, before, row)
        rows.append(row)
    return rows


def filters_kernel(picks_ref, w0, w1, w2, w3, own_ref):
    chans = w0.shape[1]
    outs = (12 * chans, 3 * chans)
    column = lax.broadcasted_iota(jnp.int32, outs, 1)
    third = (column >= chans).astype(jnp.int32) + (column >= 2 * chans).astype(jnp.int32)
    wanted = column + 3 * chans * third + chans * picks_ref[4]
    chosen = (lax.broadcasted_iota(jnp.int32, outs, 0) == wanted).astype(jnp.float32)
    chosen = chosen.astype(own_ref.dtype)
    for b in range(3):
        taps = []
        for a in range(3):
            rows = [w[3 * a + b].astype(jnp.float32) for w in (w0, w1, w2, w3)]
            rows = jnp.concatenate(rows, axis=0).astype(own_ref.dtype)
            taps.append(jnp.dot(rows, chosen, preferred_element_type=jnp.float32))
        own_ref[b] = jnp.concatenate(taps, axis=1).astype(own_ref.dtype)


def ordered(third, near, own, far):
    orders = ((own, far, near), (near, own, far), (far, near, own))
    return jnp.concatenate(
        [jnp.where(third == 0, a, jnp.where(third == 1, b, c)) for a, b, c in zip(*orders)],
        axis=0,
    )


def build_kernel(third_ref, *refs):
    g_refs, x_refs, (shifted_ref, window_ref, ends_ref) = refs[:3], refs[3:7], refs[7:]
    chans = g_refs[0].shape[0]
    rows = g_refs[0].shape[1] // WIDTH
    third = third_ref[0]
    kind = shifted_ref.dtype
    blank = jnp.zeros((9 * chans, 2 * LANES), kind)
    shifted_ref[:, : 2 * LANES] = blank
    shifted_ref[:, (rows + 2) * LANES :] = blank
    lane, lane_x = lane_index(3 * chans), lane_index(4 * chans)
    ends = jnp.zeros((4 * chans, LANES), jnp.float32)
    for start in range(0, rows, 4):
        cuts = [pl.ds((3 * start // 4 + i) * LANES, LANES) for i in range(3)]
        tiles = [ordered(third, *[g[:, cut].astype(jnp.float32) for g in g_refs]) for cut in cuts]
        for i, row in enumerate(load_rows(tiles, 2)):
            row = jnp.where((lane >= 2) & (lane < WIDTH + 2), row, 0.0)
            taps = [pltpu.roll(row, LANES - 4, 1), pltpu.roll(row, LANES - 2, 1), row]
            at = (start + i + 2) * LANES
            shifted_ref[:, at : at + LANES] = jnp.concatenate(taps, axis=0).astype(kind)
        tiles = [
            jnp.concatenate([x[:, cut].astype(jnp.float32) for x in x_refs], axis=0)
            for cut in cuts
        ]
        for i, row in enumerate(load_rows(tiles, 0)):
            r = start + i
            row = jnp.where(lane_x < WIDTH, row, 0.0)
            window_ref[:, r * LANES : (r + 1) * LANES] = row.astype(kind)
            turned = pltpu.roll(row, 4 * r, 1) if r else row
            tail = (4 * r + TAIL) % LANES
            here = (lane_x >= 4 * r) & (lane_x < 4 * r + 2)
            here = here | ((lane_x >= tail) & (lane_x < tail + 2))
            ends = jnp.where(here, turned, ends)
    ends_ref[...] = ends.astype(kind)


def weights_kernel(
    third_ref, shifted_ref, window_ref, ends_ref, left_ref, right_ref, parts_ref, borders_ref
):
    chans = left_ref.shape[0] // 3
    rows = window_ref.shape[1] // LANES
    lane = lane_index(3 * chans)
    at_head = lane % 4 < 2
    row_of = jnp.where(at_head, lane, (lane + LANES - TAIL) % LANES) // 4
    sides = [
        ordered(third_ref[0], *[ref[m * chans : (m + 1) * chans].astype(jnp.float32) for m in range(3)])
        for ref in (left_ref, right_ref)
    ]
    contract = (((1,), (1,)), ((), ()))
    for b in range(3):
        valid = (row_of >= 2 * (b - 1)) & (row_of < rows + 2 * (b - 1))
        left, right = [pltpu.roll(side, (8 * (b - 1)) % LANES, 1) if b != 1 else side for side in sides]
        left = jnp.where(valid & at_head, left, 0.0)
        right = jnp.where(valid & ~at_head, right, 0.0)
        border = jnp.concatenate([right, jnp.zeros_like(left), left], axis=0)
        borders_ref[b] = border.astype(borders_ref.dtype)
        at = (4 - 2 * b) * LANES
        part = lax.dot_general(
            window_ref[...],
            shifted_ref[:, at : at + rows * LANES],
            contract,
            preferred_element_type=jnp.float32,
        )
        part = part + lax.dot_general(
            ends_ref[...],
            border.astype(borders_ref.dtype),
            contract,
            preferred_element_type=jnp.float32,
        )
        part = jnp.concatenate([part, jnp.zeros((4 * chans, 5 * 8), jnp.float32)], axis=1)
        for j in range(4):
            for h in range(2):
                parts_ref[2 * j + h, b * chans : (b + 1) * chans] = part[
                    j * chans : (j + 1) * chans, h * LANES : (h + 1) * LANES
                ]


def inputs_kernel(shifted_ref, filters_ref, borders_ref, *out_refs):
    chans = out_refs[0].shape[0]
    rows = out_refs[0].shape[1] // WIDTH
    lane = lane_index(4 * chans)
    total, edge = None, None
    for b in range(3):
        at = (4 - 2 * b) * LANES
        part = jnp.dot(
            filters_ref[b],
            shifted_ref[:, at : at + rows * LANES],
            preferred_element_type=jnp.float32,
        )
        rim = jnp.dot(filters_ref[b], borders_ref[b], preferred_element_type=jnp.float32)
        total = part if total is None else total + part
        edge = rim if edge is None else edge + rim
    on_rim = (lane < 2) | ((lane >= TAIL) & (lane < WIDTH))
    for start in range(0, rows, 4):
        group = []
        for r in range(start, start + 4):
            rim = pltpu.roll(edge, LANES - 4 * r, 1) if r else edge
            group.append(total[:, r * LANES : (r + 1) * LANES] + jnp.where(on_rim, rim, 0.0))
        for j in range(4):
            cut = slice(j * chans, (j + 1) * chans)
            store_dense(out_refs[j], start, [row[cut] for row in group])


def total_kernel(a_ref, b_ref, c_ref, d_ref, out_ref):
    for start in range(0, out_ref.shape[1], 4):
        tiles = []
        for i in range(3):
            at = pl.ds((3 * start // 4 + i) * LANES, LANES)
            tiles.append((a_ref[:, at] + b_ref[:, at]) + (c_ref[:, at] + d_ref[:, at]))
        for i, row in enumerate(load_rows(tiles, 0)):
            out_ref[:, start + i, :] = row[:, :WIDTH]


def copies_kernel(in_ref, out_ref):
    piece = in_ref[0]
    for i in range(1, in_ref.shape[0]):
        piece = piece + in_ref[i]
    for i in range(out_ref.shape[0]):
        out_ref[i] = piece


def place_kernel(factor, layer_ref, whole_ref, out_ref):
    chans = out_ref.shape[1]
    layer = layer_ref[0]
    for b in range(3):
        rows = []
        for v in range(4):
            j = lax.rem(layer + 5 - v, 4)
            rows.append(
                jnp.concatenate(
                    [whole_ref[2 * j + h, b * chans : (b + 1) * chans] for h in range(2)], axis=1
                )
            )
        for a in range(3):
            pieces = []
            for m in range(3):
                at = (3 * a + m) * chans
                pieces += [rows[v][:, at : at + chans] for v in range(4)]
            out_ref[3 * a + b] = jnp.concatenate(pieces, axis=1) * factor


def call(kernel, outs, ins, scalars=0, scratch=()):
    return pl.pallas_call(
        kernel,
        out_shape=outs,
        in_specs=[SMEM] * scalars + [VMEM] * (ins - scalars),
        out_specs=jax.tree.map(lambda _: VMEM, outs),
        scratch_shapes=list(scratch),
        compiler_params=pltpu.CompilerParams(vmem_limit_bytes=40 << 20),
    )


def per_device(field, grad_out, filters):
    across, along = group_lists()
    spaces = lax.axis_size("space")
    chans = lax.axis_size("chan")
    chan_dev, width, rows = field.shape
    factor = 1.0 / math.sqrt(rows * width * spaces)
    layer = lax.axis_index("chan")
    kind, wide = field.dtype, jnp.float32

    def shape(*dims, dtype=kind):
        return jax.ShapeDtypeStruct(dims, dtype)

    def move(cells, step):
        return lax.ppermute(cells, "chan", [(i, (i + step) % chans) for i in range(chans)])

    def exchange(parts, groups):
        return lax.all_to_all(parts, "space", 0, 0, axis_index_groups=groups, tiled=True)

    def added(parts, copies):
        return call(copies_kernel, shape(copies, *parts.shape[1:], dtype=wide), 1)(parts)

    def by_row(cells):
        return jnp.pad(cells.transpose(2, 0, 1), ((0, 0), (0, 0), (0, LANES - width)))

    cells = rows * width
    dense = call(pack_kernel, shape(chan_dev, cells), 1)(by_row(grad_out))
    grads = [move(dense, 4), dense, move(dense, -4)]
    source = call(pack_kernel, shape(chan_dev, cells), 1)(by_row(field))
    sources = [move(source, 1), source, move(source, -1), move(source, -2)]
    edges = call(edges_kernel, shape(3 * chan_dev, LANES), 3)(*grads)
    left = lax.ppermute(edges, "space", [(i, i + 1) for i in range(spaces - 1)])
    right = lax.ppermute(edges, "space", [(i + 1, i) for i in range(spaces - 1)])

    beyond = jnp.where(lax.axis_index("space") % NCORE == 0, layer + 2, layer + chans - 2)
    blocks = [layer + chans - 1, layer, layer + 1, beyond]
    picks = jnp.stack([block % chans for block in blocks] + [layer % 4]).astype(jnp.int32)
    own = pl.pallas_call(
        filters_kernel,
        out_shape=shape(3, 4 * chan_dev, 9 * chan_dev),
        grid_spec=pltpu.PrefetchScalarGridSpec(
            num_scalar_prefetch=1,
            grid=(1,),
            in_specs=[
                pl.BlockSpec((9, chan_dev, 12 * chan_dev), lambda i, at, j=j: (0, at[j], 0))
                for j in range(4)
            ],
            out_specs=pl.BlockSpec((3, 4 * chan_dev, 9 * chan_dev), lambda i, at: (0, 0, 0)),
        ),
    )(picks, filters, filters, filters, filters)

    third = (layer // 4)[None]
    shifted, window, ends = call(
        build_kernel,
        (
            shape(9 * chan_dev, (rows + 4) * LANES),
            shape(4 * chan_dev, rows * LANES),
            shape(4 * chan_dev, LANES),
        ),
        8,
        1,
    )(third, *grads, *sources)
    parts, borders = call(
        weights_kernel,
        (shape(8, 3 * chan_dev, LANES, dtype=wide), shape(3, 9 * chan_dev, LANES)),
        6,
        1,
    )(third, shifted, window, ends, left, right)
    blocks = call(inputs_kernel, (shape(chan_dev, cells, dtype=wide),) * 4, 3)(
        shifted, own, borders
    )

    piece = added(exchange(parts, across), 1)
    piece, *blocks = lax.optimization_barrier((piece, *blocks))
    home = [
        (s * chans + c, s * chans + (c - 1 + s // (NY * NCORE)) % chans)
        for s in range(spaces)
        for c in range(chans)
    ]
    piece = lax.ppermute(piece, ("space", "chan"), home)
    apart = [
        (s * chans + c, s * chans + (c + (-2 if s % NCORE else 2)) % chans)
        for s in range(spaces)
        for c in range(chans)
    ]
    others = [
        lax.ppermute(blocks[3], ("space", "chan"), apart),
        move(blocks[0], -1),
        move(blocks[2], 1),
    ]
    piece = added(exchange(added(piece, 8), along), 8)
    whole = exchange(piece, across)
    grad_filters = call(
        functools.partial(place_kernel, factor),
        shape(9, chan_dev, 12 * chan_dev, dtype=wide),
        2,
        1,
    )(layer[None], whole)
    total = call(total_kernel, shape(chan_dev, rows, width, dtype=wide), 4)(blocks[1], *others)
    return (total.transpose(0, 2, 1), grad_filters)


def solution(mesh):
    in_specs = (P("chan", "space", None), P("chan", "space", None), P())
    out_specs = (P("chan", "space", None), P(None, "chan", None))
    return jax.shard_map(
        per_device, mesh=mesh, in_specs=in_specs, out_specs=out_specs, check_vma=False
    )
```

```python
import functools
import math

import jax
import jax.numpy as jnp
from jax import lax
from jax.experimental import pallas as pl
from jax.experimental.pallas import tpu as pltpu
from jax.sharding import PartitionSpec as P

NX, NY, NCORE = 4, 8, 2
LANES, WIDTH = 128, 96
TAIL = WIDTH - 2
VMEM = pl.BlockSpec(memory_space=pltpu.VMEM)
SMEM = pl.BlockSpec(memory_space=pltpu.SMEM)


def group_lists():
    def at(x, y, core):
        return (x * NY + y) * NCORE + core

    across = [[at(x, y, c) for x in range(NX) for c in range(NCORE)] for y in range(NY)]
    along = [[at(x, y, c) for y in range(NY)] for x in range(NX) for c in range(NCORE)]
    return across, along


def lane_index(chans):
    return lax.broadcasted_iota(jnp.int32, (chans, LANES), 1)


def pack_kernel(cells_ref, dense_ref):
    for start in range(0, cells_ref.shape[0], 4):
        store_dense(dense_ref, start, [cells_ref[start + i].astype(jnp.float32) for i in range(4)])


def edges_kernel(near_ref, own_ref, far_ref, edges_ref):
    refs = (near_ref, own_ref, far_ref)
    rows = near_ref.shape[1] // WIDTH
    lane = lane_index(3 * near_ref.shape[0])
    packed = jnp.zeros(edges_ref.shape, jnp.float32)
    for r in range(rows):
        for column, to in ((TAIL, 4 * r), (0, (4 * r + TAIL) % LANES)):
            tile, at = divmod(r * WIDTH + column, LANES)
            cut = slice(tile * LANES, (tile + 1) * LANES)
            block = jnp.concatenate([ref[:, cut].astype(jnp.float32) for ref in refs], axis=0)
            turn = (to - at) % LANES
            block = pltpu.roll(block, turn, 1) if turn else block
            packed = jnp.where((lane >= to) & (lane < to + 2), block, packed)
    edges_ref[...] = packed.astype(edges_ref.dtype)


def store_dense(dense_ref, start, group):
    lane = lane_index(group[0].shape[0])
    turned = [group[0]] + [pltpu.roll(group[i], LANES - 32 * i, 1) for i in (1, 2, 3)]
    tiles = [jnp.where(lane < LANES - 32 * (i + 1), turned[i], turned[i + 1]) for i in range(3)]
    for i in range(3):
        at = (3 * start // 4 + i) * LANES
        dense_ref[:, at : at + LANES] = tiles[i].astype(dense_ref.dtype)


def load_rows(tiles, offset):
    lane = lane_index(tiles[0].shape[0])
    rows = []
    for i in range(4):
        turn = (32 * i + offset) % LANES
        row = pltpu.roll(tiles[min(i, 2)], turn, 1) if turn else tiles[i]
        if i in (1, 2):
            before = pltpu.roll(tiles[i - 1], turn, 1)
            row = jnp.where(lane < 32 * i + offset, before, row)
        rows.append(row)
    return rows


def window_block(j, code):
    layer, core = code // 2, code % 2
    step = (11, 0, 1, 2 + 8 * core)[j]
    return (layer + step) % 12


def filters_kernel(code_ref, w0, w1, w2, w3, own_ref):
    chans = w0.shape[1]
    outs = (12 * chans, 3 * chans)
    column = lax.broadcasted_iota(jnp.int32, outs, 1)
    third = (column >= chans).astype(jnp.int32) + (column >= 2 * chans).astype(jnp.int32)
    wanted = column + 3 * chans * third + chans * ((code_ref[0] // 2) % 4)
    chosen = (lax.broadcasted_iota(jnp.int32, outs, 0) == wanted).astype(jnp.float32)
    chosen = chosen.astype(own_ref.dtype)
    picked = []
    for w in (w0, w1, w2, w3):
        flat = w[...].reshape(9 * chans, 12 * chans)
        picked.append(jnp.dot(flat, chosen, preferred_element_type=jnp.float32))
    for b in range(3):
        taps = []
        for a in range(3):
            cut = slice((3 * a + b) * chans, (3 * a + b + 1) * chans)
            taps.append(jnp.concatenate([rows[cut] for rows in picked], axis=0))
        own_ref[b] = jnp.concatenate(taps, axis=1).astype(own_ref.dtype)


def ordered(third, near, own, far):
    orders = ((own, far, near), (near, own, far), (far, near, own))
    return jnp.concatenate(
        [jnp.where(third == 0, a, jnp.where(third == 1, b, c)) for a, b, c in zip(*orders)],
        axis=0,
    )


def build_kernel(third_ref, *refs):
    g_refs, (x3, x2, x0, x1), (shifted_ref, window_ref, ends_ref) = refs[:3], refs[3:7], refs[8:]
    x_refs = (x0, x1, x2, x3)
    chans = g_refs[0].shape[0]
    rows = g_refs[0].shape[1] // WIDTH
    third = third_ref[0]
    kind = shifted_ref.dtype
    blank = jnp.zeros((9 * chans, 2 * LANES), kind)
    shifted_ref[:, : 2 * LANES] = blank
    shifted_ref[:, (rows + 2) * LANES :] = blank
    lane, lane_x = lane_index(3 * chans), lane_index(4 * chans)
    ends = jnp.zeros((4 * chans, LANES), jnp.float32)
    for start in range(0, rows, 4):
        cuts = [pl.ds((3 * start // 4 + i) * LANES, LANES) for i in range(3)]
        tiles = [ordered(third, *[g[:, cut].astype(jnp.float32) for g in g_refs]) for cut in cuts]
        for i, row in enumerate(load_rows(tiles, 2)):
            row = jnp.where((lane >= 2) & (lane < WIDTH + 2), row, 0.0)
            taps = [pltpu.roll(row, LANES - 4, 1), pltpu.roll(row, LANES - 2, 1), row]
            at = (start + i + 2) * LANES
            shifted_ref[:, at : at + LANES] = jnp.concatenate(taps, axis=0).astype(kind)
        tiles = [
            jnp.concatenate([x[:, cut].astype(jnp.float32) for x in x_refs], axis=0)
            for cut in cuts
        ]
        for i, row in enumerate(load_rows(tiles, 0)):
            r = start + i
            row = jnp.where(lane_x < WIDTH, row, 0.0)
            window_ref[:, r * LANES : (r + 1) * LANES] = row.astype(kind)
            turned = pltpu.roll(row, 4 * r, 1) if r else row
            tail = (4 * r + TAIL) % LANES
            here = (lane_x >= 4 * r) & (lane_x < 4 * r + 2)
            here = here | ((lane_x >= tail) & (lane_x < tail + 2))
            ends = jnp.where(here, turned, ends)
    ends_ref[...] = ends.astype(kind)


def weights_kernel(
    third_ref, shifted_ref, window_ref, ends_ref, left_ref, right_ref, parts_ref, borders_ref
):
    chans = left_ref.shape[0] // 3
    rows = window_ref.shape[1] // LANES
    lane = lane_index(3 * chans)
    at_head = lane % 4 < 2
    row_of = jnp.where(at_head, lane, (lane + LANES - TAIL) % LANES) // 4
    sides = [
        ordered(third_ref[0], *[ref[m * chans : (m + 1) * chans].astype(jnp.float32) for m in range(3)])
        for ref in (left_ref, right_ref)
    ]
    contract = (((1,), (1,)), ((), ()))
    for b in range(3):
        valid = (row_of >= 2 * (b - 1)) & (row_of < rows + 2 * (b - 1))
        left, right = [pltpu.roll(side, (8 * (b - 1)) % LANES, 1) if b != 1 else side for side in sides]
        left = jnp.where(valid & at_head, left, 0.0)
        right = jnp.where(valid & ~at_head, right, 0.0)
        border = jnp.concatenate([right, jnp.zeros_like(left), left], axis=0)
        borders_ref[b] = border.astype(borders_ref.dtype)
        at = (4 - 2 * b) * LANES
        part = lax.dot_general(
            window_ref[...],
            shifted_ref[:, at : at + rows * LANES],
            contract,
            preferred_element_type=jnp.float32,
        )
        part = part + lax.dot_general(
            ends_ref[...],
            border.astype(borders_ref.dtype),
            contract,
            preferred_element_type=jnp.float32,
        )
        part = jnp.concatenate([part, jnp.zeros((4 * chans, 5 * 8), jnp.float32)], axis=1)
        for j in range(4):
            for h in range(2):
                parts_ref[2 * j + h, b * chans : (b + 1) * chans] = part[
                    j * chans : (j + 1) * chans, h * LANES : (h + 1) * LANES
                ]


def inputs_kernel(shifted_ref, filters_ref, borders_ref, *out_refs):
    chans = out_refs[0].shape[0]
    rows = out_refs[0].shape[1] // WIDTH
    lane = lane_index(4 * chans)
    total, edge = None, None
    for b in range(3):
        at = (4 - 2 * b) * LANES
        part = jnp.dot(
            filters_ref[b],
            shifted_ref[:, at : at + rows * LANES],
            preferred_element_type=jnp.float32,
        )
        rim = jnp.dot(filters_ref[b], borders_ref[b], preferred_element_type=jnp.float32)
        total = part if total is None else total + part
        edge = rim if edge is None else edge + rim
    on_rim = (lane < 2) | ((lane >= TAIL) & (lane < WIDTH))
    for start in range(0, rows, 4):
        group = []
        for r in range(start, start + 4):
            rim = pltpu.roll(edge, LANES - 4 * r, 1) if r else edge
            group.append(total[:, r * LANES : (r + 1) * LANES] + jnp.where(on_rim, rim, 0.0))
        for j in range(4):
            cut = slice(j * chans, (j + 1) * chans)
            store_dense(out_refs[j], start, [row[cut] for row in group])


def total_kernel(a_ref, b_ref, c_ref, d_ref, out_ref):
    for start in range(0, out_ref.shape[1], 4):
        tiles = []
        for i in range(3):
            at = pl.ds((3 * start // 4 + i) * LANES, LANES)
            tiles.append((a_ref[:, at] + b_ref[:, at]) + (c_ref[:, at] + d_ref[:, at]))
        for i, row in enumerate(load_rows(tiles, 0)):
            out_ref[:, start + i, :] = row[:, :WIDTH]


def copies_kernel(in_ref, out_ref):
    piece = in_ref[0]
    for i in range(1, in_ref.shape[0]):
        piece = piece + in_ref[i]
    for i in range(out_ref.shape[0]):
        out_ref[i] = piece


def place_kernel(factor, layer_ref, whole_ref, out_ref):
    chans = out_ref.shape[1]
    layer = layer_ref[0]
    for b in range(3):
        rows = []
        for v in range(4):
            j = lax.rem(layer + 5 - v, 4)
            rows.append(
                jnp.concatenate(
                    [whole_ref[2 * j + h, b * chans : (b + 1) * chans] for h in range(2)], axis=1
                )
            )
        for a in range(3):
            pieces = []
            for m in range(3):
                at = (3 * a + m) * chans
                pieces += [rows[v][:, at : at + chans] for v in range(4)]
            out_ref[3 * a + b] = jnp.concatenate(pieces, axis=1) * factor


def call(kernel, outs, ins, scalars=0, scratch=()):
    return pl.pallas_call(
        kernel,
        out_shape=outs,
        in_specs=[SMEM] * scalars + [VMEM] * (ins - scalars),
        out_specs=jax.tree.map(lambda _: VMEM, outs),
        scratch_shapes=list(scratch),
        compiler_params=pltpu.CompilerParams(vmem_limit_bytes=40 << 20),
    )


def per_device(field, grad_out, filters):
    across, along = group_lists()
    spaces = lax.axis_size("space")
    chans = lax.axis_size("chan")
    chan_dev, width, rows = field.shape
    factor = 1.0 / math.sqrt(rows * width * spaces)
    layer = lax.axis_index("chan")
    kind, wide = field.dtype, jnp.float32

    def shape(*dims, dtype=kind):
        return jax.ShapeDtypeStruct(dims, dtype)

    def move(cells, step):
        return lax.ppermute(cells, "chan", [(i, (i + step) % chans) for i in range(chans)])

    def exchange(parts, groups):
        return lax.all_to_all(parts, "space", 0, 0, axis_index_groups=groups, tiled=True)

    def added(parts, copies):
        return call(copies_kernel, shape(copies, *parts.shape[1:], dtype=wide), 1)(parts)

    def by_row(cells):
        return jnp.pad(cells.transpose(2, 0, 1), ((0, 0), (0, 0), (0, LANES - width)))

    cells = rows * width
    dense = call(pack_kernel, shape(chan_dev, cells), 1)(by_row(grad_out))
    grads = [move(dense, 4), dense, move(dense, -4)]
    source = call(pack_kernel, shape(chan_dev, cells), 1)(by_row(field))
    sources = [move(source, 1), source, move(source, -1), move(source, -2)]
    edges = call(edges_kernel, shape(3 * chan_dev, LANES), 3)(*grads)
    left = lax.ppermute(edges, "space", [(i, i + 1) for i in range(spaces - 1)])
    right = lax.ppermute(edges, "space", [(i + 1, i) for i in range(spaces - 1)])

    code = (2 * layer + lax.axis_index("space") % NCORE)[None]
    own = pl.pallas_call(
        filters_kernel,
        out_shape=shape(3, 4 * chan_dev, 9 * chan_dev),
        grid_spec=pltpu.PrefetchScalarGridSpec(
            num_scalar_prefetch=1,
            grid=(1,),
            in_specs=[
                pl.BlockSpec((9, chan_dev, 12 * chan_dev), lambda i, at, j=j: (0, window_block(j, at[0]), 0))
                for j in range(4)
            ],
            out_specs=pl.BlockSpec((3, 4 * chan_dev, 9 * chan_dev), lambda i, at: (0, 0, 0)),
        ),
    )(code, filters, filters, filters, filters)

    third = (layer // 4)[None]
    shifted, window, ends = call(
        build_kernel,
        (
            shape(9 * chan_dev, (rows + 4) * LANES),
            shape(4 * chan_dev, rows * LANES),
            shape(4 * chan_dev, LANES),
        ),
        9,
        1,
    )(third, *grads, sources[3], sources[2], sources[0], sources[1], own)
    parts, borders = call(
        weights_kernel,
        (shape(8, 3 * chan_dev, LANES, dtype=wide), shape(3, 9 * chan_dev, LANES)),
        6,
        1,
    )(third, shifted, window, ends, left, right)
    blocks = call(inputs_kernel, (shape(chan_dev, cells, dtype=wide),) * 4, 3)(
        shifted, own, borders
    )

    piece = added(exchange(parts, across), 1)
    piece, *blocks = lax.optimization_barrier((piece, *blocks))
    home = [
        (s * chans + c, s * chans + (c - 1 + s // (NY * NCORE)) % chans)
        for s in range(spaces)
        for c in range(chans)
    ]
    piece = lax.ppermute(piece, ("space", "chan"), home)
    apart = [
        (s * chans + c, s * chans + (c + (-2 if s % NCORE else 2)) % chans)
        for s in range(spaces)
        for c in range(chans)
    ]
    others = [
        lax.ppermute(blocks[3], ("space", "chan"), apart),
        move(blocks[0], -1),
        move(blocks[2], 1),
    ]
    piece = added(exchange(added(piece, 8), along), 8)
    whole = exchange(piece, across)
    grad_filters = call(
        functools.partial(place_kernel, factor),
        shape(9, chan_dev, 12 * chan_dev, dtype=wide),
        2,
        1,
    )(layer[None], whole)
    total = call(total_kernel, shape(chan_dev, rows, width, dtype=wide), 4)(blocks[1], *others)
    return (total.transpose(0, 2, 1), grad_filters)


def solution(mesh):
    in_specs = (P("chan", "space", None), P("chan", "space", None), P())
    out_specs = (P("chan", "space", None), P(None, "chan", None))
    return jax.shard_map(
        per_device, mesh=mesh, in_specs=in_specs, out_specs=out_specs, check_vma=False
    )
```

```python
import functools
import math

import jax
import jax.numpy as jnp
from jax import lax
from jax.experimental import pallas as pl
from jax.experimental.pallas import tpu as pltpu
from jax.sharding import PartitionSpec as P

NX, NY, NCORE = 4, 8, 2
LANES, WIDTH = 128, 96
TAIL = WIDTH - 2
VMEM = pl.BlockSpec(memory_space=pltpu.VMEM)
SMEM = pl.BlockSpec(memory_space=pltpu.SMEM)


def group_lists():
    def at(x, y, core):
        return (x * NY + y) * NCORE + core

    across = [[at(x, y, c) for x in range(NX) for c in range(NCORE)] for y in range(NY)]
    along = [[at(x, y, c) for y in range(NY)] for x in range(NX) for c in range(NCORE)]
    return across, along


def lane_index(chans):
    return lax.broadcasted_iota(jnp.int32, (chans, LANES), 1)


def pack_kernel(cells_ref, dense_ref):
    chans, rows, width = cells_ref.shape
    for start in range(0, rows, 8):
        block = cells_ref[:, start : start + 8, :].astype(jnp.float32)
        block = jnp.concatenate(
            [block, jnp.zeros((chans, 8, LANES - width), jnp.float32)], axis=2
        )
        block = jnp.swapaxes(block, 0, 1)
        for half in (0, 4):
            store_dense(dense_ref, start + half, [block[half + i] for i in range(4)])


def edges_kernel(near_ref, own_ref, far_ref, edges_ref):
    refs = (near_ref, own_ref, far_ref)
    rows = near_ref.shape[1] // WIDTH
    lane = lane_index(3 * near_ref.shape[0])
    packed = jnp.zeros(edges_ref.shape, jnp.float32)
    for r in range(rows):
        for column, to in ((TAIL, 4 * r), (0, (4 * r + TAIL) % LANES)):
            tile, at = divmod(r * WIDTH + column, LANES)
            cut = slice(tile * LANES, (tile + 1) * LANES)
            block = jnp.concatenate([ref[:, cut].astype(jnp.float32) for ref in refs], axis=0)
            turn = (to - at) % LANES
            block = pltpu.roll(block, turn, 1) if turn else block
            packed = jnp.where((lane >= to) & (lane < to + 2), block, packed)
    edges_ref[...] = packed.astype(edges_ref.dtype)


def store_dense(dense_ref, start, group):
    lane = lane_index(group[0].shape[0])
    turned = [group[0]] + [pltpu.roll(group[i], LANES - 32 * i, 1) for i in (1, 2, 3)]
    tiles = [jnp.where(lane < LANES - 32 * (i + 1), turned[i], turned[i + 1]) for i in range(3)]
    for i in range(3):
        at = (3 * start // 4 + i) * LANES
        dense_ref[:, at : at + LANES] = tiles[i].astype(dense_ref.dtype)


def load_rows(tiles, offset):
    lane = lane_index(tiles[0].shape[0])
    rows = []
    for i in range(4):
        turn = (32 * i + offset) % LANES
        row = pltpu.roll(tiles[min(i, 2)], turn, 1) if turn else tiles[i]
        if i in (1, 2):
            before = pltpu.roll(tiles[i - 1], turn, 1)
            row = jnp.where(lane < 32 * i + offset, before, row)
        rows.append(row)
    return rows


def window_block(j, code):
    layer, core = code // 2, code % 2
    step = (11, 0, 1, 2 + 8 * core)[j]
    return (layer + step) % 12


def filters_kernel(code_ref, w0, w1, w2, w3, own_ref, token_ref):
    chans = w0.shape[1]
    outs = (12 * chans, 3 * chans)
    column = lax.broadcasted_iota(jnp.int32, outs, 1)
    third = (column >= chans).astype(jnp.int32) + (column >= 2 * chans).astype(jnp.int32)
    wanted = column + 3 * chans * third + chans * ((code_ref[0] // 2) % 4)
    chosen = (lax.broadcasted_iota(jnp.int32, outs, 0) == wanted).astype(jnp.float32)
    chosen = chosen.astype(own_ref.dtype)
    token_ref[...] = jnp.zeros(token_ref.shape, token_ref.dtype)
    picked = []
    for w in (w0, w1, w2, w3):
        flat = w[...].reshape(9 * chans, 12 * chans)
        picked.append(jnp.dot(flat, chosen, preferred_element_type=jnp.float32))
    for b in range(3):
        taps = []
        for a in range(3):
            cut = slice((3 * a + b) * chans, (3 * a + b + 1) * chans)
            taps.append(jnp.concatenate([rows[cut] for rows in picked], axis=0))
        own_ref[b] = jnp.concatenate(taps, axis=1).astype(own_ref.dtype)


def ordered(third, near, own, far):
    orders = ((own, far, near), (near, own, far), (far, near, own))
    return jnp.concatenate(
        [jnp.where(third == 0, a, jnp.where(third == 1, b, c)) for a, b, c in zip(*orders)],
        axis=0,
    )


def build_kernel(third_ref, *refs):
    g_refs, (x3, x2, x0, x1), (shifted_ref, window_ref, ends_ref) = refs[:3], refs[3:7], refs[8:]
    x_refs = (x0, x1, x2, x3)
    chans = g_refs[0].shape[0]
    rows = g_refs[0].shape[1] // WIDTH
    third = third_ref[0]
    kind = shifted_ref.dtype
    blank = jnp.zeros((9 * chans, 2 * LANES), kind)
    shifted_ref[:, : 2 * LANES] = blank
    shifted_ref[:, (rows + 2) * LANES :] = blank
    lane, lane_x = lane_index(3 * chans), lane_index(4 * chans)
    ends = jnp.zeros((4 * chans, LANES), jnp.float32)
    for start in range(0, rows, 4):
        cuts = [pl.ds((3 * start // 4 + i) * LANES, LANES) for i in range(3)]
        tiles = [ordered(third, *[g[:, cut].astype(jnp.float32) for g in g_refs]) for cut in cuts]
        for i, row in enumerate(load_rows(tiles, 2)):
            row = jnp.where((lane >= 2) & (lane < WIDTH + 2), row, 0.0)
            taps = [pltpu.roll(row, LANES - 4, 1), pltpu.roll(row, LANES - 2, 1), row]
            at = (start + i + 2) * LANES
            shifted_ref[:, at : at + LANES] = jnp.concatenate(taps, axis=0).astype(kind)
        tiles = [
            jnp.concatenate([x[:, cut].astype(jnp.float32) for x in x_refs], axis=0)
            for cut in cuts
        ]
        for i, row in enumerate(load_rows(tiles, 0)):
            r = start + i
            row = jnp.where(lane_x < WIDTH, row, 0.0)
            window_ref[:, r * LANES : (r + 1) * LANES] = row.astype(kind)
            turned = pltpu.roll(row, 4 * r, 1) if r else row
            tail = (4 * r + TAIL) % LANES
            here = (lane_x >= 4 * r) & (lane_x < 4 * r + 2)
            here = here | ((lane_x >= tail) & (lane_x < tail + 2))
            ends = jnp.where(here, turned, ends)
    ends_ref[...] = ends.astype(kind)


def weights_kernel(
    third_ref, shifted_ref, window_ref, ends_ref, left_ref, right_ref, parts_ref, borders_ref
):
    chans = left_ref.shape[0] // 3
    rows = window_ref.shape[1] // LANES
    lane = lane_index(3 * chans)
    at_head = lane % 4 < 2
    row_of = jnp.where(at_head, lane, (lane + LANES - TAIL) % LANES) // 4
    sides = [
        ordered(third_ref[0], *[ref[m * chans : (m + 1) * chans].astype(jnp.float32) for m in range(3)])
        for ref in (left_ref, right_ref)
    ]
    contract = (((1,), (1,)), ((), ()))
    for b in range(3):
        valid = (row_of >= 2 * (b - 1)) & (row_of < rows + 2 * (b - 1))
        left, right = [pltpu.roll(side, (8 * (b - 1)) % LANES, 1) if b != 1 else side for side in sides]
        left = jnp.where(valid & at_head, left, 0.0)
        right = jnp.where(valid & ~at_head, right, 0.0)
        border = jnp.concatenate([right, jnp.zeros_like(left), left], axis=0)
        borders_ref[b] = border.astype(borders_ref.dtype)
        at = (4 - 2 * b) * LANES
        part = lax.dot_general(
            window_ref[...],
            shifted_ref[:, at : at + rows * LANES],
            contract,
            preferred_element_type=jnp.float32,
        )
        part = part + lax.dot_general(
            ends_ref[...],
            border.astype(borders_ref.dtype),
            contract,
            preferred_element_type=jnp.float32,
        )
        part = jnp.concatenate([part, jnp.zeros((4 * chans, 5 * 8), jnp.float32)], axis=1)
        for j in range(4):
            for h in range(2):
                parts_ref[2 * j + h, b * chans : (b + 1) * chans] = part[
                    j * chans : (j + 1) * chans, h * LANES : (h + 1) * LANES
                ]


def inputs_kernel(shifted_ref, filters_ref, borders_ref, *out_refs):
    chans = out_refs[0].shape[0]
    rows = out_refs[0].shape[1] // WIDTH
    lane = lane_index(4 * chans)
    total, edge = None, None
    for b in range(3):
        at = (4 - 2 * b) * LANES
        part = jnp.dot(
            filters_ref[b],
            shifted_ref[:, at : at + rows * LANES],
            preferred_element_type=jnp.float32,
        )
        rim = jnp.dot(filters_ref[b], borders_ref[b], preferred_element_type=jnp.float32)
        total = part if total is None else total + part
        edge = rim if edge is None else edge + rim
    on_rim = (lane < 2) | ((lane >= TAIL) & (lane < WIDTH))
    for start in range(0, rows, 4):
        group = []
        for r in range(start, start + 4):
            rim = pltpu.roll(edge, LANES - 4 * r, 1) if r else edge
            group.append(total[:, r * LANES : (r + 1) * LANES] + jnp.where(on_rim, rim, 0.0))
        for j in range(4):
            cut = slice(j * chans, (j + 1) * chans)
            store_dense(out_refs[j], start, [row[cut] for row in group])


def total_kernel(a_ref, b_ref, c_ref, d_ref, out_ref):
    for start in range(0, out_ref.shape[1], 4):
        tiles = []
        for i in range(3):
            at = pl.ds((3 * start // 4 + i) * LANES, LANES)
            tiles.append((a_ref[:, at] + b_ref[:, at]) + (c_ref[:, at] + d_ref[:, at]))
        for i, row in enumerate(load_rows(tiles, 0)):
            out_ref[:, start + i, :] = row[:, :WIDTH]


def copies_kernel(in_ref, out_ref):
    piece = in_ref[0]
    for i in range(1, in_ref.shape[0]):
        piece = piece + in_ref[i]
    for i in range(out_ref.shape[0]):
        out_ref[i] = piece


def place_kernel(factor, layer_ref, whole_ref, out_ref):
    chans = out_ref.shape[1]
    layer = layer_ref[0]
    for b in range(3):
        rows = []
        for v in range(4):
            j = lax.rem(layer + 5 - v, 4)
            rows.append(
                jnp.concatenate(
                    [whole_ref[2 * j + h, b * chans : (b + 1) * chans] for h in range(2)], axis=1
                )
            )
        for a in range(3):
            pieces = []
            for m in range(3):
                at = (3 * a + m) * chans
                pieces += [rows[v][:, at : at + chans] for v in range(4)]
            out_ref[3 * a + b] = jnp.concatenate(pieces, axis=1) * factor


def call(kernel, outs, ins, scalars=0, scratch=()):
    return pl.pallas_call(
        kernel,
        out_shape=outs,
        in_specs=[SMEM] * scalars + [VMEM] * (ins - scalars),
        out_specs=jax.tree.map(lambda _: VMEM, outs),
        scratch_shapes=list(scratch),
        compiler_params=pltpu.CompilerParams(vmem_limit_bytes=40 << 20),
    )


def per_device(field, grad_out, filters):
    across, along = group_lists()
    spaces = lax.axis_size("space")
    chans = lax.axis_size("chan")
    chan_dev, width, rows = field.shape
    factor = 1.0 / math.sqrt(rows * width * spaces)
    layer = lax.axis_index("chan")
    kind, wide = field.dtype, jnp.float32

    def shape(*dims, dtype=kind):
        return jax.ShapeDtypeStruct(dims, dtype)

    def move(cells, step):
        return lax.ppermute(cells, "chan", [(i, (i + step) % chans) for i in range(chans)])

    def exchange(parts, groups):
        return lax.all_to_all(parts, "space", 0, 0, axis_index_groups=groups, tiled=True)

    def added(parts, copies):
        return call(copies_kernel, shape(copies, *parts.shape[1:], dtype=wide), 1)(parts)

    def by_row(cells):
        return cells.transpose(0, 2, 1)

    cells = rows * width
    dense = call(pack_kernel, shape(chan_dev, cells), 1)(by_row(grad_out))
    grads = [move(dense, 4), dense, move(dense, -4)]
    source = call(pack_kernel, shape(chan_dev, cells), 1)(by_row(field))
    sources = [move(source, 1), source, move(source, -1), move(source, -2)]
    edges = call(edges_kernel, shape(3 * chan_dev, LANES), 3)(*grads)
    left = lax.ppermute(edges, "space", [(i, i + 1) for i in range(spaces - 1)])
    right = lax.ppermute(edges, "space", [(i + 1, i) for i in range(spaces - 1)])

    code = (2 * layer + lax.axis_index("space") % NCORE)[None]
    own, token = pl.pallas_call(
        filters_kernel,
        out_shape=(shape(3, 4 * chan_dev, 9 * chan_dev), shape(8, LANES, dtype=wide)),
        grid_spec=pltpu.PrefetchScalarGridSpec(
            num_scalar_prefetch=1,
            grid=(1,),
            in_specs=[
                pl.BlockSpec((9, chan_dev, 12 * chan_dev), lambda i, at, j=j: (0, window_block(j, at[0]), 0))
                for j in range(4)
            ],
            out_specs=(
                pl.BlockSpec((3, 4 * chan_dev, 9 * chan_dev), lambda i, at: (0, 0, 0)),
                pl.BlockSpec((8, LANES), lambda i, at: (0, 0)),
            ),
        ),
    )(code, filters, filters, filters, filters)

    third = (layer // 4)[None]
    shifted, window, ends = call(
        build_kernel,
        (
            shape(9 * chan_dev, (rows + 4) * LANES),
            shape(4 * chan_dev, rows * LANES),
            shape(4 * chan_dev, LANES),
        ),
        9,
        1,
    )(third, *grads, sources[3], sources[2], sources[0], sources[1], token)
    parts, borders = call(
        weights_kernel,
        (shape(8, 3 * chan_dev, LANES, dtype=wide), shape(3, 9 * chan_dev, LANES)),
        6,
        1,
    )(third, shifted, window, ends, left, right)
    blocks = call(inputs_kernel, (shape(chan_dev, cells, dtype=wide),) * 4, 3)(
        shifted, own, borders
    )

    piece = added(exchange(parts, across), 1)
    piece, *blocks = lax.optimization_barrier((piece, *blocks))
    home = [
        (s * chans + c, s * chans + (c - 1 + s // (NY * NCORE)) % chans)
        for s in range(spaces)
        for c in range(chans)
    ]
    piece = lax.ppermute(piece, ("space", "chan"), home)
    apart = [
        (s * chans + c, s * chans + (c + (-2 if s % NCORE else 2)) % chans)
        for s in range(spaces)
        for c in range(chans)
    ]
    others = [
        lax.ppermute(blocks[3], ("space", "chan"), apart),
        move(blocks[0], -1),
        move(blocks[2], 1),
    ]
    piece = added(exchange(added(piece, 8), along), 8)
    whole = exchange(piece, across)
    grad_filters = call(
        functools.partial(place_kernel, factor),
        shape(9, chan_dev, 12 * chan_dev, dtype=wide),
        2,
        1,
    )(layer[None], whole)
    total = call(total_kernel, shape(chan_dev, rows, width, dtype=wide), 4)(blocks[1], *others)
    return (total.transpose(0, 2, 1), grad_filters)


def solution(mesh):
    in_specs = (P("chan", "space", None), P("chan", "space", None), P())
    out_specs = (P("chan", "space", None), P(None, "chan", None))
    return jax.shard_map(
        per_device, mesh=mesh, in_specs=in_specs, out_specs=out_specs, check_vma=False
    )
```

```python
import functools
import math

import jax
import jax.numpy as jnp
from jax import lax
from jax.experimental import pallas as pl
from jax.experimental.pallas import tpu as pltpu
from jax.sharding import PartitionSpec as P

NX, NY, NCORE = 4, 8, 2
LANES, WIDTH = 128, 96
TAIL = WIDTH - 2
VMEM = pl.BlockSpec(memory_space=pltpu.VMEM)
SMEM = pl.BlockSpec(memory_space=pltpu.SMEM)


def group_lists():
    def at(x, y, core):
        return (x * NY + y) * NCORE + core

    across = [[at(x, y, c) for x in range(NX) for c in range(NCORE)] for y in range(NY)]
    along = [[at(x, y, c) for y in range(NY)] for x in range(NX) for c in range(NCORE)]
    return across, along


def lane_index(chans):
    return lax.broadcasted_iota(jnp.int32, (chans, LANES), 1)


def pack_kernel(cells_ref, dense_ref):
    chans, rows, width = cells_ref.shape
    blank = jnp.zeros((chans, 8, LANES - width), jnp.float32)
    for start in range(0, rows, 8):
        block = cells_ref[:, start : start + 8, :].astype(jnp.float32)
        block = jnp.swapaxes(jnp.concatenate([block, blank], axis=2), 0, 1)
        for half in (0, 4):
            store_dense(dense_ref, start + half, [block[half + i] for i in range(4)])


def sorted_blocks(code, first, own, second):
    even = code % 2 == 0
    return jnp.where(even, first, second), own, jnp.where(even, second, first)


def edges_kernel(code_ref, first_ref, own_ref, second_ref, edges_ref):
    refs = (first_ref, own_ref, second_ref)
    code = code_ref[0]
    rows = own_ref.shape[1] // WIDTH
    lane = lane_index(3 * own_ref.shape[0])
    packed = jnp.zeros(edges_ref.shape, jnp.float32)
    for r in range(rows):
        for column, to in ((TAIL, 4 * r), (0, (4 * r + TAIL) % LANES)):
            tile, at = divmod(r * WIDTH + column, LANES)
            cut = slice(tile * LANES, (tile + 1) * LANES)
            block = [ref[:, cut].astype(jnp.float32) for ref in refs]
            block = jnp.concatenate(sorted_blocks(code, *block), axis=0)
            turn = (to - at) % LANES
            block = pltpu.roll(block, turn, 1) if turn else block
            packed = jnp.where((lane >= to) & (lane < to + 2), block, packed)
    edges_ref[...] = packed.astype(edges_ref.dtype)


def store_dense(dense_ref, start, group):
    lane = lane_index(group[0].shape[0])
    turned = [group[0]] + [pltpu.roll(group[i], LANES - 32 * i, 1) for i in (1, 2, 3)]
    tiles = [jnp.where(lane < LANES - 32 * (i + 1), turned[i], turned[i + 1]) for i in range(3)]
    for i in range(3):
        at = (3 * start // 4 + i) * LANES
        dense_ref[:, at : at + LANES] = tiles[i].astype(dense_ref.dtype)


def load_rows(tiles, offset):
    lane = lane_index(tiles[0].shape[0])
    rows = []
    for i in range(4):
        turn = (32 * i + offset) % LANES
        row = pltpu.roll(tiles[min(i, 2)], turn, 1) if turn else tiles[i]
        if i in (1, 2):
            before = pltpu.roll(tiles[i - 1], turn, 1)
            row = jnp.where(lane < 32 * i + offset, before, row)
        rows.append(row)
    return rows


def window_block(j, code):
    layer, core = code // 2, code % 2
    step = (11, 0, 1, 2 + 8 * core)[j]
    return (layer + step) % 12


def filters_kernel(code_ref, w0, w1, w2, w3, own_ref):
    chans = w0.shape[1]
    outs = (12 * chans, 3 * chans)
    column = lax.broadcasted_iota(jnp.int32, outs, 1)
    third = (column >= chans).astype(jnp.int32) + (column >= 2 * chans).astype(jnp.int32)
    wanted = column + 3 * chans * third + chans * ((code_ref[0] // 2) % 4)
    chosen = (lax.broadcasted_iota(jnp.int32, outs, 0) == wanted).astype(jnp.float32)
    chosen = chosen.astype(own_ref.dtype)
    picked = []
    for w in (w0, w1, w2, w3):
        flat = w[...].reshape(9 * chans, 12 * chans)
        picked.append(jnp.dot(flat, chosen, preferred_element_type=jnp.float32))
    for b in range(3):
        taps = []
        for a in range(3):
            cut = slice((3 * a + b) * chans, (3 * a + b + 1) * chans)
            taps.append(jnp.concatenate([rows[cut] for rows in picked], axis=0))
        own_ref[b] = jnp.concatenate(taps, axis=1).astype(own_ref.dtype)


def ordered(code, near, own, far):
    third = code // 8
    orders = ((own, far, near), (near, own, far), (far, near, own))
    return jnp.concatenate(
        [jnp.where(third == 0, a, jnp.where(third == 1, b, c)) for a, b, c in zip(*orders)],
        axis=0,
    )


def build_kernel(code_ref, *refs):
    g_refs, (x3, x2, x0, x1), (shifted_ref, window_ref, ends_ref) = refs[:3], refs[3:7], refs[7:]
    x_refs = (x0, x1, x2, x3)
    chans = g_refs[0].shape[0]
    rows = g_refs[0].shape[1] // WIDTH
    code = code_ref[0]
    kind = shifted_ref.dtype
    blank = jnp.zeros((9 * chans, 2 * LANES), kind)
    shifted_ref[:, : 2 * LANES] = blank
    shifted_ref[:, (rows + 2) * LANES :] = blank
    lane, lane_x = lane_index(3 * chans), lane_index(4 * chans)
    ends = jnp.zeros((4 * chans, LANES), jnp.float32)
    for start in range(0, rows, 4):
        cuts = [pl.ds((3 * start // 4 + i) * LANES, LANES) for i in range(3)]
        tiles = [[g[:, cut].astype(jnp.float32) for g in g_refs] for cut in cuts]
        tiles = [ordered(code, *sorted_blocks(code, *blocks)) for blocks in tiles]
        for i, row in enumerate(load_rows(tiles, 2)):
            row = jnp.where((lane >= 2) & (lane < WIDTH + 2), row, 0.0)
            taps = [pltpu.roll(row, LANES - 4, 1), pltpu.roll(row, LANES - 2, 1), row]
            at = (start + i + 2) * LANES
            shifted_ref[:, at : at + LANES] = jnp.concatenate(taps, axis=0).astype(kind)
        tiles = [
            jnp.concatenate([x[:, cut].astype(jnp.float32) for x in x_refs], axis=0)
            for cut in cuts
        ]
        for i, row in enumerate(load_rows(tiles, 0)):
            r = start + i
            row = jnp.where(lane_x < WIDTH, row, 0.0)
            window_ref[:, r * LANES : (r + 1) * LANES] = row.astype(kind)
            turned = pltpu.roll(row, 4 * r, 1) if r else row
            tail = (4 * r + TAIL) % LANES
            here = (lane_x >= 4 * r) & (lane_x < 4 * r + 2)
            here = here | ((lane_x >= tail) & (lane_x < tail + 2))
            ends = jnp.where(here, turned, ends)
    ends_ref[...] = ends.astype(kind)


def weights_kernel(
    code_ref, shifted_ref, window_ref, ends_ref, left_ref, right_ref, parts_ref, borders_ref
):
    chans = left_ref.shape[0] // 3
    rows = window_ref.shape[1] // LANES
    lane = lane_index(3 * chans)
    at_head = lane % 4 < 2
    row_of = jnp.where(at_head, lane, (lane + LANES - TAIL) % LANES) // 4
    sides = [
        ordered(code_ref[0], *[ref[m * chans : (m + 1) * chans].astype(jnp.float32) for m in range(3)])
        for ref in (left_ref, right_ref)
    ]
    contract = (((1,), (1,)), ((), ()))
    for b in range(3):
        valid = (row_of >= 2 * (b - 1)) & (row_of < rows + 2 * (b - 1))
        left, right = [pltpu.roll(side, (8 * (b - 1)) % LANES, 1) if b != 1 else side for side in sides]
        left = jnp.where(valid & at_head, left, 0.0)
        right = jnp.where(valid & ~at_head, right, 0.0)
        border = jnp.concatenate([right, jnp.zeros_like(left), left], axis=0)
        borders_ref[b] = border.astype(borders_ref.dtype)
        at = (4 - 2 * b) * LANES
        part = lax.dot_general(
            window_ref[...],
            shifted_ref[:, at : at + rows * LANES],
            contract,
            preferred_element_type=jnp.float32,
        )
        part = part + lax.dot_general(
            ends_ref[...],
            border.astype(borders_ref.dtype),
            contract,
            preferred_element_type=jnp.float32,
        )
        part = jnp.concatenate([part, jnp.zeros((4 * chans, 5 * 8), jnp.float32)], axis=1)
        for j in range(4):
            for h in range(2):
                parts_ref[2 * j + h, b * chans : (b + 1) * chans] = part[
                    j * chans : (j + 1) * chans, h * LANES : (h + 1) * LANES
                ]


def inputs_kernel(shifted_ref, filters_ref, borders_ref, *out_refs):
    chans = out_refs[0].shape[0]
    rows = out_refs[0].shape[1] // WIDTH
    lane = lane_index(4 * chans)
    total, edge = None, None
    for b in range(3):
        at = (4 - 2 * b) * LANES
        part = jnp.dot(
            filters_ref[b],
            shifted_ref[:, at : at + rows * LANES],
            preferred_element_type=jnp.float32,
        )
        rim = jnp.dot(filters_ref[b], borders_ref[b], preferred_element_type=jnp.float32)
        total = part if total is None else total + part
        edge = rim if edge is None else edge + rim
    on_rim = (lane < 2) | ((lane >= TAIL) & (lane < WIDTH))
    for start in range(0, rows, 4):
        group = []
        for r in range(start, start + 4):
            rim = pltpu.roll(edge, LANES - 4 * r, 1) if r else edge
            group.append(total[:, r * LANES : (r + 1) * LANES] + jnp.where(on_rim, rim, 0.0))
        for j in range(4):
            cut = slice(j * chans, (j + 1) * chans)
            store_dense(out_refs[j], start, [row[cut] for row in group])


def total_kernel(a_ref, b_ref, c_ref, d_ref, out_ref):
    for start in range(0, out_ref.shape[1], 4):
        tiles = []
        for i in range(3):
            at = pl.ds((3 * start // 4 + i) * LANES, LANES)
            tiles.append((a_ref[:, at] + b_ref[:, at]) + (c_ref[:, at] + d_ref[:, at]))
        for i, row in enumerate(load_rows(tiles, 0)):
            out_ref[:, start + i, :] = row[:, :WIDTH]


def copies_kernel(in_ref, out_ref):
    piece = in_ref[0]
    for i in range(1, in_ref.shape[0]):
        piece = piece + in_ref[i]
    for i in range(out_ref.shape[0]):
        out_ref[i] = piece


def place_kernel(factor, layer_ref, whole_ref, out_ref):
    chans = out_ref.shape[1]
    layer = layer_ref[0]
    for b in range(3):
        rows = []
        for v in range(4):
            j = lax.rem(layer + 5 - v, 4)
            rows.append(
                jnp.concatenate(
                    [whole_ref[2 * j + h, b * chans : (b + 1) * chans] for h in range(2)], axis=1
                )
            )
        for a in range(3):
            pieces = []
            for m in range(3):
                at = (3 * a + m) * chans
                pieces += [rows[v][:, at : at + chans] for v in range(4)]
            out_ref[3 * a + b] = jnp.concatenate(pieces, axis=1) * factor


def call(kernel, outs, ins, scalars=0, scratch=()):
    return pl.pallas_call(
        kernel,
        out_shape=outs,
        in_specs=[SMEM] * scalars + [VMEM] * (ins - scalars),
        out_specs=jax.tree.map(lambda _: VMEM, outs),
        scratch_shapes=list(scratch),
        compiler_params=pltpu.CompilerParams(vmem_limit_bytes=40 << 20),
    )


def per_device(field, grad_out, filters):
    across, along = group_lists()
    spaces = lax.axis_size("space")
    chans = lax.axis_size("chan")
    chan_dev, width, rows = field.shape
    factor = 1.0 / math.sqrt(rows * width * spaces)
    layer = lax.axis_index("chan")
    kind, wide = field.dtype, jnp.float32

    def shape(*dims, dtype=kind):
        return jax.ShapeDtypeStruct(dims, dtype)

    def move(cells, step):
        return lax.ppermute(cells, "chan", [(i, (i + step) % chans) for i in range(chans)])

    def exchange(parts, groups):
        return lax.all_to_all(parts, "space", 0, 0, axis_index_groups=groups, tiled=True)

    def added(parts, copies):
        return call(copies_kernel, shape(copies, *parts.shape[1:], dtype=wide), 1)(parts)

    def by_row(cells):
        return cells.transpose(0, 2, 1)

    cells = rows * width
    code = (2 * layer + lax.axis_index("space") % NCORE)[None]
    dense = call(pack_kernel, shape(chan_dev, cells), 1)(by_row(grad_out))
    source = call(pack_kernel, shape(chan_dev, cells), 1)(by_row(field))

    def apart(cells, even, odd):
        pairs = [
            (s * chans + c, s * chans + (c + (odd if s % NCORE else even)) % chans)
            for s in range(spaces)
            for c in range(chans)
        ]
        return lax.ppermute(cells, ("space", "chan"), pairs)

    grads = [apart(dense, 4, -4), dense, apart(dense, -4, 4)]
    sources = [move(source, 1), source, move(source, -1), move(source, -2)]
    edges = call(edges_kernel, shape(3 * chan_dev, LANES), 4, 1)(code, *grads)
    left = lax.ppermute(edges, "space", [(i, i + 1) for i in range(spaces - 1)])
    right = lax.ppermute(edges, "space", [(i + 1, i) for i in range(spaces - 1)])

    own = pl.pallas_call(
        filters_kernel,
        out_shape=shape(3, 4 * chan_dev, 9 * chan_dev),
        grid_spec=pltpu.PrefetchScalarGridSpec(
            num_scalar_prefetch=1,
            grid=(1,),
            in_specs=[
                pl.BlockSpec((9, chan_dev, 12 * chan_dev), lambda i, at, j=j: (0, window_block(j, at[0]), 0))
                for j in range(4)
            ],
            out_specs=pl.BlockSpec((3, 4 * chan_dev, 9 * chan_dev), lambda i, at: (0, 0, 0)),
        ),
    )(code, filters, filters, filters, filters)

    shifted, window, ends = call(
        build_kernel,
        (
            shape(9 * chan_dev, (rows + 4) * LANES),
            shape(4 * chan_dev, rows * LANES),
            shape(4 * chan_dev, LANES),
        ),
        8,
        1,
    )(code, *grads, sources[3], sources[2], sources[0], sources[1])
    parts, borders = call(
        weights_kernel,
        (shape(8, 3 * chan_dev, LANES, dtype=wide), shape(3, 9 * chan_dev, LANES)),
        6,
        1,
    )(code, shifted, window, ends, left, right)
    blocks = call(inputs_kernel, (shape(chan_dev, cells, dtype=wide),) * 4, 3)(
        shifted, own, borders
    )

    piece = added(exchange(parts, across), 1)
    piece, *blocks = lax.optimization_barrier((piece, *blocks))
    home = [
        (s * chans + c, s * chans + (c - 1 + s // (NY * NCORE)) % chans)
        for s in range(spaces)
        for c in range(chans)
    ]
    piece = lax.ppermute(piece, ("space", "chan"), home)
    others = [apart(blocks[3], 2, -2), move(blocks[0], -1), move(blocks[2], 1)]
    piece = added(exchange(added(piece, 8), along), 8)
    whole = exchange(piece, across)
    grad_filters = call(
        functools.partial(place_kernel, factor),
        shape(9, chan_dev, 12 * chan_dev, dtype=wide),
        2,
        1,
    )(layer[None], whole)
    total = call(total_kernel, shape(chan_dev, rows, width, dtype=wide), 4)(blocks[1], *others)
    return (total.transpose(0, 2, 1), grad_filters)


def solution(mesh):
    in_specs = (P("chan", "space", None), P("chan", "space", None), P())
    out_specs = (P("chan", "space", None), P(None, "chan", None))
    return jax.shard_map(
        per_device, mesh=mesh, in_specs=in_specs, out_specs=out_specs, check_vma=False
    )
```

```python
import functools
import math

import jax
import jax.numpy as jnp
from jax import lax
from jax.experimental import pallas as pl
from jax.experimental.pallas import tpu as pltpu
from jax.sharding import PartitionSpec as P

NX, NY, NCORE = 4, 8, 2
LANES, WIDTH = 128, 96
TAIL = WIDTH - 2
VMEM = pl.BlockSpec(memory_space=pltpu.VMEM)
SMEM = pl.BlockSpec(memory_space=pltpu.SMEM)


def group_lists():
    def at(x, y, core):
        return (x * NY + y) * NCORE + core

    across = [[at(x, y, c) for x in range(NX) for c in range(NCORE)] for y in range(NY)]
    along = [[at(x, y, c) for y in range(NY)] for x in range(NX) for c in range(NCORE)]
    return across, along


def lane_index(chans):
    return lax.broadcasted_iota(jnp.int32, (chans, LANES), 1)


def pack_kernel(cells_ref, dense_ref):
    chans, rows, width = cells_ref.shape
    blank = jnp.zeros((chans, 8, LANES - width), jnp.float32)
    for start in range(0, rows, 8):
        block = cells_ref[:, start : start + 8, :].astype(jnp.float32)
        block = jnp.swapaxes(jnp.concatenate([block, blank], axis=2), 0, 1)
        for half in (0, 4):
            store_dense(dense_ref, start + half, [block[half + i] for i in range(4)])


def sorted_blocks(code, first, own, second):
    even = code % 2 == 0
    return jnp.where(even, first, second), own, jnp.where(even, second, first)


def edges_kernel(code_ref, first_ref, own_ref, second_ref, edges_ref):
    refs = (first_ref, own_ref, second_ref)
    code = code_ref[0]
    rows = own_ref.shape[1] // WIDTH
    lane = lane_index(3 * own_ref.shape[0])
    packed = jnp.zeros(edges_ref.shape, jnp.float32)
    for r in range(rows):
        for column, to in ((TAIL, 4 * r), (0, (4 * r + TAIL) % LANES)):
            tile, at = divmod(r * WIDTH + column, LANES)
            cut = slice(tile * LANES, (tile + 1) * LANES)
            block = [ref[:, cut].astype(jnp.float32) for ref in refs]
            block = jnp.concatenate(sorted_blocks(code, *block), axis=0)
            turn = (to - at) % LANES
            block = pltpu.roll(block, turn, 1) if turn else block
            packed = jnp.where((lane >= to) & (lane < to + 2), block, packed)
    edges_ref[...] = packed.astype(edges_ref.dtype)


def store_dense(dense_ref, start, group):
    lane = lane_index(group[0].shape[0])
    turned = [group[0]] + [pltpu.roll(group[i], LANES - 32 * i, 1) for i in (1, 2, 3)]
    tiles = [jnp.where(lane < LANES - 32 * (i + 1), turned[i], turned[i + 1]) for i in range(3)]
    for i in range(3):
        at = (3 * start // 4 + i) * LANES
        dense_ref[:, at : at + LANES] = tiles[i].astype(dense_ref.dtype)


def load_rows(tiles, offset):
    lane = lane_index(tiles[0].shape[0])
    rows = []
    for i in range(4):
        turn = (32 * i + offset) % LANES
        row = pltpu.roll(tiles[min(i, 2)], turn, 1) if turn else tiles[i]
        if i in (1, 2):
            before = pltpu.roll(tiles[i - 1], turn, 1)
            row = jnp.where(lane < 32 * i + offset, before, row)
        rows.append(row)
    return rows


def window_block(j, code):
    layer, core = code // 2, code % 2
    step = (11, 0, 1, 2 + 8 * core)[j]
    return (layer + step) % 12


def filters_kernel(code_ref, w0, w1, w2, w3, own_ref):
    chans = w0.shape[1]
    outs = (12 * chans, 3 * chans)
    column = lax.broadcasted_iota(jnp.int32, outs, 1)
    third = (column >= chans).astype(jnp.int32) + (column >= 2 * chans).astype(jnp.int32)
    wanted = column + 3 * chans * third + chans * ((code_ref[0] // 2) % 4)
    chosen = (lax.broadcasted_iota(jnp.int32, outs, 0) == wanted).astype(jnp.float32)
    chosen = chosen.astype(own_ref.dtype)
    picked = []
    for w in (w0, w1, w2, w3):
        flat = w[...].reshape(9 * chans, 12 * chans)
        picked.append(jnp.dot(flat, chosen, preferred_element_type=jnp.float32))
    for b in range(3):
        taps = []
        for a in range(3):
            cut = slice((3 * a + b) * chans, (3 * a + b + 1) * chans)
            taps.append(jnp.concatenate([rows[cut] for rows in picked], axis=0))
        own_ref[b] = jnp.concatenate(taps, axis=1).astype(own_ref.dtype)


def ordered(code, near, own, far):
    third = code // 8
    orders = ((own, far, near), (near, own, far), (far, near, own))
    return jnp.concatenate(
        [jnp.where(third == 0, a, jnp.where(third == 1, b, c)) for a, b, c in zip(*orders)],
        axis=0,
    )


def build_kernel(code_ref, *refs):
    g_refs, x_refs, (shifted_ref, window_ref, ends_ref) = refs[:3], refs[3:7], refs[7:]
    chans = g_refs[0].shape[0]
    rows = g_refs[0].shape[1] // WIDTH
    code = code_ref[0]
    kind = shifted_ref.dtype
    blank = jnp.zeros((9 * chans, 2 * LANES), kind)
    shifted_ref[:, : 2 * LANES] = blank
    shifted_ref[:, (rows + 2) * LANES :] = blank
    lane, lane_x = lane_index(3 * chans), lane_index(4 * chans)
    ends = jnp.zeros((4 * chans, LANES), jnp.float32)
    for start in range(0, rows, 4):
        cuts = [pl.ds((3 * start // 4 + i) * LANES, LANES) for i in range(3)]
        tiles = [[g[:, cut].astype(jnp.float32) for g in g_refs] for cut in cuts]
        tiles = [ordered(code, *sorted_blocks(code, *blocks)) for blocks in tiles]
        for i, row in enumerate(load_rows(tiles, 2)):
            row = jnp.where((lane >= 2) & (lane < WIDTH + 2), row, 0.0)
            taps = [pltpu.roll(row, LANES - 4, 1), pltpu.roll(row, LANES - 2, 1), row]
            at = (start + i + 2) * LANES
            shifted_ref[:, at : at + LANES] = jnp.concatenate(taps, axis=0).astype(kind)
        tiles = []
        for cut in cuts:
            outer, second, first, own = [x[:, cut].astype(jnp.float32) for x in x_refs]
            near = sorted_blocks(code, first, own, second)
            tiles.append(jnp.concatenate([*near, outer], axis=0))
        for i, row in enumerate(load_rows(tiles, 0)):
            r = start + i
            row = jnp.where(lane_x < WIDTH, row, 0.0)
            window_ref[:, r * LANES : (r + 1) * LANES] = row.astype(kind)
            turned = pltpu.roll(row, 4 * r, 1) if r else row
            tail = (4 * r + TAIL) % LANES
            here = (lane_x >= 4 * r) & (lane_x < 4 * r + 2)
            here = here | ((lane_x >= tail) & (lane_x < tail + 2))
            ends = jnp.where(here, turned, ends)
    ends_ref[...] = ends.astype(kind)


def weights_kernel(
    code_ref, shifted_ref, window_ref, ends_ref, left_ref, right_ref, parts_ref, borders_ref
):
    chans = left_ref.shape[0] // 3
    rows = window_ref.shape[1] // LANES
    lane = lane_index(3 * chans)
    at_head = lane % 4 < 2
    row_of = jnp.where(at_head, lane, (lane + LANES - TAIL) % LANES) // 4
    sides = [
        ordered(code_ref[0], *[ref[m * chans : (m + 1) * chans].astype(jnp.float32) for m in range(3)])
        for ref in (left_ref, right_ref)
    ]
    contract = (((1,), (1,)), ((), ()))
    for b in range(3):
        valid = (row_of >= 2 * (b - 1)) & (row_of < rows + 2 * (b - 1))
        left, right = [pltpu.roll(side, (8 * (b - 1)) % LANES, 1) if b != 1 else side for side in sides]
        left = jnp.where(valid & at_head, left, 0.0)
        right = jnp.where(valid & ~at_head, right, 0.0)
        border = jnp.concatenate([right, jnp.zeros_like(left), left], axis=0)
        borders_ref[b] = border.astype(borders_ref.dtype)
        at = (4 - 2 * b) * LANES
        part = lax.dot_general(
            window_ref[...],
            shifted_ref[:, at : at + rows * LANES],
            contract,
            preferred_element_type=jnp.float32,
        )
        part = part + lax.dot_general(
            ends_ref[...],
            border.astype(borders_ref.dtype),
            contract,
            preferred_element_type=jnp.float32,
        )
        part = jnp.concatenate([part, jnp.zeros((4 * chans, 5 * 8), jnp.float32)], axis=1)
        for j in range(4):
            for h in range(2):
                parts_ref[2 * j + h, b * chans : (b + 1) * chans] = part[
                    j * chans : (j + 1) * chans, h * LANES : (h + 1) * LANES
                ]


def inputs_kernel(code_ref, shifted_ref, filters_ref, borders_ref, *out_refs):
    chans = out_refs[0].shape[0]
    rows = out_refs[0].shape[1] // WIDTH
    lane = lane_index(4 * chans)
    total, edge = None, None
    for b in range(3):
        at = (4 - 2 * b) * LANES
        part = jnp.dot(
            filters_ref[b],
            shifted_ref[:, at : at + rows * LANES],
            preferred_element_type=jnp.float32,
        )
        rim = jnp.dot(filters_ref[b], borders_ref[b], preferred_element_type=jnp.float32)
        total = part if total is None else total + part
        edge = rim if edge is None else edge + rim
    on_rim = (lane < 2) | ((lane >= TAIL) & (lane < WIDTH))
    for start in range(0, rows, 4):
        group = []
        for r in range(start, start + 4):
            rim = pltpu.roll(edge, LANES - 4 * r, 1) if r else edge
            group.append(total[:, r * LANES : (r + 1) * LANES] + jnp.where(on_rim, rim, 0.0))
        blocks = [[row[j * chans : (j + 1) * chans] for j in range(4)] for row in group]
        blocks = [[*sorted_blocks(code_ref[0], *row[:3]), row[3]] for row in blocks]
        for j in range(4):
            store_dense(out_refs[j], start, [row[j] for row in blocks])


def total_kernel(a_ref, b_ref, c_ref, d_ref, out_ref):
    for start in range(0, out_ref.shape[1], 4):
        tiles = []
        for i in range(3):
            at = pl.ds((3 * start // 4 + i) * LANES, LANES)
            tiles.append((a_ref[:, at] + b_ref[:, at]) + (c_ref[:, at] + d_ref[:, at]))
        for i, row in enumerate(load_rows(tiles, 0)):
            out_ref[:, start + i, :] = row[:, :WIDTH]


def copies_kernel(in_ref, out_ref):
    piece = in_ref[0]
    for i in range(1, in_ref.shape[0]):
        piece = piece + in_ref[i]
    for i in range(out_ref.shape[0]):
        out_ref[i] = piece


def place_kernel(factor, layer_ref, whole_ref, out_ref):
    chans = out_ref.shape[1]
    layer = layer_ref[0]
    for b in range(3):
        rows = []
        for v in range(4):
            j = lax.rem(layer + 5 - v, 4)
            rows.append(
                jnp.concatenate(
                    [whole_ref[2 * j + h, b * chans : (b + 1) * chans] for h in range(2)], axis=1
                )
            )
        for a in range(3):
            pieces = []
            for m in range(3):
                at = (3 * a + m) * chans
                pieces += [rows[v][:, at : at + chans] for v in range(4)]
            out_ref[3 * a + b] = jnp.concatenate(pieces, axis=1) * factor


def call(kernel, outs, ins, scalars=0, scratch=()):
    return pl.pallas_call(
        kernel,
        out_shape=outs,
        in_specs=[SMEM] * scalars + [VMEM] * (ins - scalars),
        out_specs=jax.tree.map(lambda _: VMEM, outs),
        scratch_shapes=list(scratch),
        compiler_params=pltpu.CompilerParams(vmem_limit_bytes=40 << 20),
    )


def per_device(field, grad_out, filters):
    across, along = group_lists()
    spaces = lax.axis_size("space")
    chans = lax.axis_size("chan")
    chan_dev, width, rows = field.shape
    factor = 1.0 / math.sqrt(rows * width * spaces)
    layer = lax.axis_index("chan")
    kind, wide = field.dtype, jnp.float32

    def shape(*dims, dtype=kind):
        return jax.ShapeDtypeStruct(dims, dtype)

    def move(cells, step):
        return lax.ppermute(cells, "chan", [(i, (i + step) % chans) for i in range(chans)])

    def exchange(parts, groups):
        return lax.all_to_all(parts, "space", 0, 0, axis_index_groups=groups, tiled=True)

    def added(parts, copies):
        return call(copies_kernel, shape(copies, *parts.shape[1:], dtype=wide), 1)(parts)

    def by_row(cells):
        return cells.transpose(0, 2, 1)

    cells = rows * width
    code = (2 * layer + lax.axis_index("space") % NCORE)[None]
    dense = call(pack_kernel, shape(chan_dev, cells), 1)(by_row(grad_out))
    source = call(pack_kernel, shape(chan_dev, cells), 1)(by_row(field))

    def apart(cells, even, odd):
        pairs = [
            (s * chans + c, s * chans + (c + (odd if s % NCORE else even)) % chans)
            for s in range(spaces)
            for c in range(chans)
        ]
        return lax.ppermute(cells, ("space", "chan"), pairs)

    grads = [apart(dense, 4, -4), dense, apart(dense, -4, 4)]
    sources = [move(source, -2), apart(source, -1, 1), apart(source, 1, -1), source]
    edges = call(edges_kernel, shape(3 * chan_dev, LANES), 4, 1)(code, *grads)
    left = lax.ppermute(edges, "space", [(i, i + 1) for i in range(spaces - 1)])
    right = lax.ppermute(edges, "space", [(i + 1, i) for i in range(spaces - 1)])

    own = pl.pallas_call(
        filters_kernel,
        out_shape=shape(3, 4 * chan_dev, 9 * chan_dev),
        grid_spec=pltpu.PrefetchScalarGridSpec(
            num_scalar_prefetch=1,
            grid=(1,),
            in_specs=[
                pl.BlockSpec((9, chan_dev, 12 * chan_dev), lambda i, at, j=j: (0, window_block(j, at[0]), 0))
                for j in range(4)
            ],
            out_specs=pl.BlockSpec((3, 4 * chan_dev, 9 * chan_dev), lambda i, at: (0, 0, 0)),
        ),
    )(code, filters, filters, filters, filters)

    shifted, window, ends = call(
        build_kernel,
        (
            shape(9 * chan_dev, (rows + 4) * LANES),
            shape(4 * chan_dev, rows * LANES),
            shape(4 * chan_dev, LANES),
        ),
        8,
        1,
    )(code, *grads, *sources)
    parts, borders = call(
        weights_kernel,
        (shape(8, 3 * chan_dev, LANES, dtype=wide), shape(3, 9 * chan_dev, LANES)),
        6,
        1,
    )(code, shifted, window, ends, left, right)
    blocks = call(inputs_kernel, (shape(chan_dev, cells, dtype=wide),) * 4, 4, 1)(
        code, shifted, own, borders
    )

    piece = added(exchange(parts, across), 1)
    piece, *blocks = lax.optimization_barrier((piece, *blocks))
    home = [
        (s * chans + c, s * chans + (c - 1 + s // (NY * NCORE)) % chans)
        for s in range(spaces)
        for c in range(chans)
    ]
    piece = lax.ppermute(piece, ("space", "chan"), home)
    others = [apart(blocks[3], 2, -2), apart(blocks[0], -1, 1), apart(blocks[2], 1, -1)]
    piece = added(exchange(added(piece, 8), along), 8)
    whole = exchange(piece, across)
    grad_filters = call(
        functools.partial(place_kernel, factor),
        shape(9, chan_dev, 12 * chan_dev, dtype=wide),
        2,
        1,
    )(layer[None], whole)
    total = call(total_kernel, shape(chan_dev, rows, width, dtype=wide), 4)(blocks[1], *others)
    return (total.transpose(0, 2, 1), grad_filters)


def solution(mesh):
    in_specs = (P("chan", "space", None), P("chan", "space", None), P())
    out_specs = (P("chan", "space", None), P(None, "chan", None))
    return jax.shard_map(
        per_device, mesh=mesh, in_specs=in_specs, out_specs=out_specs, check_vma=False
    )
```

```python
import functools
import math

import jax
import jax.numpy as jnp
from jax import lax
from jax.experimental import pallas as pl
from jax.experimental.pallas import tpu as pltpu
from jax.sharding import PartitionSpec as P

NX, NY, NCORE = 4, 8, 2
LANES, WIDTH = 128, 96
TAIL = WIDTH - 2
VMEM = pl.BlockSpec(memory_space=pltpu.VMEM)
SMEM = pl.BlockSpec(memory_space=pltpu.SMEM)


def group_lists():
    def at(x, y, core):
        return (x * NY + y) * NCORE + core

    across = [[at(x, y, c) for x in range(NX) for c in range(NCORE)] for y in range(NY)]
    along = [[at(x, y, c) for y in range(NY)] for x in range(NX) for c in range(NCORE)]
    return across, along


def lane_index(chans):
    return lax.broadcasted_iota(jnp.int32, (chans, LANES), 1)


def pack_kernel(cells_ref, dense_ref):
    chans, rows, width = cells_ref.shape
    blank = jnp.zeros((chans, 8, LANES - width), jnp.float32)
    for start in range(0, rows, 8):
        block = cells_ref[:, start : start + 8, :].astype(jnp.float32)
        block = jnp.swapaxes(jnp.concatenate([block, blank], axis=2), 0, 1)
        for half in (0, 4):
            store_dense(dense_ref, start + half, [block[half + i] for i in range(4)])


def sorted_blocks(code, first, own, second):
    even = code % 2 == 0
    return jnp.where(even, first, second), own, jnp.where(even, second, first)


def edges_kernel(code_ref, first_ref, own_ref, second_ref, edges_ref):
    refs = (first_ref, own_ref, second_ref)
    code = code_ref[0]
    rows = own_ref.shape[1] // WIDTH
    lane = lane_index(3 * own_ref.shape[0])
    packed = jnp.zeros(edges_ref.shape, jnp.float32)
    for r in range(rows):
        for column, to in ((TAIL, 4 * r), (0, (4 * r + TAIL) % LANES)):
            tile, at = divmod(r * WIDTH + column, LANES)
            cut = slice(tile * LANES, (tile + 1) * LANES)
            block = [ref[:, cut].astype(jnp.float32) for ref in refs]
            block = jnp.concatenate(sorted_blocks(code, *block), axis=0)
            turn = (to - at) % LANES
            block = pltpu.roll(block, turn, 1) if turn else block
            packed = jnp.where((lane >= to) & (lane < to + 2), block, packed)
    edges_ref[...] = packed.astype(edges_ref.dtype)


def store_dense(dense_ref, start, group):
    lane = lane_index(group[0].shape[0])
    turned = [group[0]] + [pltpu.roll(group[i], LANES - 32 * i, 1) for i in (1, 2, 3)]
    tiles = [jnp.where(lane < LANES - 32 * (i + 1), turned[i], turned[i + 1]) for i in range(3)]
    for i in range(3):
        at = (3 * start // 4 + i) * LANES
        dense_ref[:, at : at + LANES] = tiles[i].astype(dense_ref.dtype)


def load_rows(tiles, offset):
    lane = lane_index(tiles[0].shape[0])
    rows = []
    for i in range(4):
        turn = (32 * i + offset) % LANES
        row = pltpu.roll(tiles[min(i, 2)], turn, 1) if turn else tiles[i]
        if i in (1, 2):
            before = pltpu.roll(tiles[i - 1], turn, 1)
            row = jnp.where(lane < 32 * i + offset, before, row)
        rows.append(row)
    return rows


def window_block(j, code):
    layer, core = code // 2, code % 2
    step = (11, 0, 1, 2 + 8 * core)[j]
    return (layer + step) % 12


def filters_kernel(code_ref, w0, w1, w2, w3, own_ref):
    chans = w0.shape[1]
    outs = (12 * chans, 3 * chans)
    column = lax.broadcasted_iota(jnp.int32, outs, 1)
    third = (column >= chans).astype(jnp.int32) + (column >= 2 * chans).astype(jnp.int32)
    wanted = column + 3 * chans * third + chans * ((code_ref[0] // 2) % 4)
    chosen = (lax.broadcasted_iota(jnp.int32, outs, 0) == wanted).astype(jnp.float32)
    chosen = chosen.astype(own_ref.dtype)
    picked = []
    for w in (w0, w1, w2, w3):
        flat = w[...].reshape(9 * chans, 12 * chans)
        picked.append(jnp.dot(flat, chosen, preferred_element_type=jnp.float32))
    for b in range(3):
        taps = []
        for a in range(3):
            cut = slice((3 * a + b) * chans, (3 * a + b + 1) * chans)
            taps.append(jnp.concatenate([rows[cut] for rows in picked], axis=0))
        own_ref[b] = jnp.concatenate(taps, axis=1).astype(own_ref.dtype)


def ordered(code, near, own, far):
    third = code // 8
    orders = ((own, far, near), (near, own, far), (far, near, own))
    return jnp.concatenate(
        [jnp.where(third == 0, a, jnp.where(third == 1, b, c)) for a, b, c in zip(*orders)],
        axis=0,
    )


def build_kernel(code_ref, *refs):
    g_refs, x_refs, (shifted_ref, window_ref, ends_ref) = refs[:3], refs[3:7], refs[7:]
    chans = g_refs[0].shape[0]
    rows = g_refs[0].shape[1] // WIDTH
    code = code_ref[0]
    kind = shifted_ref.dtype
    blank = jnp.zeros((9 * chans, 2 * LANES), kind)
    shifted_ref[:, : 2 * LANES] = blank
    shifted_ref[:, (rows + 2) * LANES :] = blank
    lane, lane_x = lane_index(3 * chans), lane_index(4 * chans)
    ends = jnp.zeros((4 * chans, LANES), jnp.float32)
    for start in range(0, rows, 4):
        cuts = [pl.ds((3 * start // 4 + i) * LANES, LANES) for i in range(3)]
        tiles = [[g[:, cut].astype(jnp.float32) for g in g_refs] for cut in cuts]
        tiles = [ordered(code, *sorted_blocks(code, *blocks)) for blocks in tiles]
        for i, row in enumerate(load_rows(tiles, 2)):
            row = jnp.where((lane >= 2) & (lane < WIDTH + 2), row, 0.0)
            taps = [pltpu.roll(row, LANES - 4, 1), pltpu.roll(row, LANES - 2, 1), row]
            at = (start + i + 2) * LANES
            shifted_ref[:, at : at + LANES] = jnp.concatenate(taps, axis=0).astype(kind)
        tiles = []
        for cut in cuts:
            outer, second, first, own = [x[:, cut].astype(jnp.float32) for x in x_refs]
            near = sorted_blocks(code, first, own, second)
            tiles.append(jnp.concatenate([*near, outer], axis=0))
        for i, row in enumerate(load_rows(tiles, 0)):
            r = start + i
            row = jnp.where(lane_x < WIDTH, row, 0.0)
            window_ref[:, r * LANES : (r + 1) * LANES] = row.astype(kind)
            turned = pltpu.roll(row, 4 * r, 1) if r else row
            tail = (4 * r + TAIL) % LANES
            here = (lane_x >= 4 * r) & (lane_x < 4 * r + 2)
            here = here | ((lane_x >= tail) & (lane_x < tail + 2))
            ends = jnp.where(here, turned, ends)
    ends_ref[...] = ends.astype(kind)


def weights_kernel(
    code_ref, shifted_ref, window_ref, ends_ref, inner_ref, outer_ref, parts_ref, borders_ref
):
    chans = inner_ref.shape[0] // 3
    rows = window_ref.shape[1] // LANES
    lane = lane_index(3 * chans)
    at_head = lane % 4 < 2
    row_of = jnp.where(at_head, lane, (lane + LANES - TAIL) % LANES) // 4
    inner, outer = inner_ref[...].astype(jnp.float32), outer_ref[...].astype(jnp.float32)
    right, _, left = sorted_blocks(code_ref[0], inner, None, outer)
    sides = [
        ordered(code_ref[0], *[side[m * chans : (m + 1) * chans] for m in range(3)])
        for side in (left, right)
    ]
    contract = (((1,), (1,)), ((), ()))
    for b in range(3):
        valid = (row_of >= 2 * (b - 1)) & (row_of < rows + 2 * (b - 1))
        left, right = [pltpu.roll(side, (8 * (b - 1)) % LANES, 1) if b != 1 else side for side in sides]
        left = jnp.where(valid & at_head, left, 0.0)
        right = jnp.where(valid & ~at_head, right, 0.0)
        border = jnp.concatenate([right, jnp.zeros_like(left), left], axis=0)
        borders_ref[b] = border.astype(borders_ref.dtype)
        at = (4 - 2 * b) * LANES
        part = lax.dot_general(
            window_ref[...],
            shifted_ref[:, at : at + rows * LANES],
            contract,
            preferred_element_type=jnp.float32,
        )
        part = part + lax.dot_general(
            ends_ref[...],
            border.astype(borders_ref.dtype),
            contract,
            preferred_element_type=jnp.float32,
        )
        part = jnp.concatenate([part, jnp.zeros((4 * chans, 5 * 8), jnp.float32)], axis=1)
        for j in range(4):
            for h in range(2):
                parts_ref[2 * j + h, b * chans : (b + 1) * chans] = part[
                    j * chans : (j + 1) * chans, h * LANES : (h + 1) * LANES
                ]


def inputs_kernel(code_ref, shifted_ref, filters_ref, borders_ref, *out_refs):
    chans = out_refs[0].shape[0]
    rows = out_refs[0].shape[1] // WIDTH
    lane = lane_index(4 * chans)
    total, edge = None, None
    for b in range(3):
        at = (4 - 2 * b) * LANES
        part = jnp.dot(
            filters_ref[b],
            shifted_ref[:, at : at + rows * LANES],
            preferred_element_type=jnp.float32,
        )
        rim = jnp.dot(filters_ref[b], borders_ref[b], preferred_element_type=jnp.float32)
        total = part if total is None else total + part
        edge = rim if edge is None else edge + rim
    on_rim = (lane < 2) | ((lane >= TAIL) & (lane < WIDTH))
    for start in range(0, rows, 4):
        group = []
        for r in range(start, start + 4):
            rim = pltpu.roll(edge, LANES - 4 * r, 1) if r else edge
            group.append(total[:, r * LANES : (r + 1) * LANES] + jnp.where(on_rim, rim, 0.0))
        blocks = [[row[j * chans : (j + 1) * chans] for j in range(4)] for row in group]
        blocks = [[*sorted_blocks(code_ref[0], *row[:3]), row[3]] for row in blocks]
        for j in range(4):
            store_dense(out_refs[j], start, [row[j] for row in blocks])


def total_kernel(a_ref, b_ref, c_ref, d_ref, out_ref):
    for start in range(0, out_ref.shape[1], 4):
        tiles = []
        for i in range(3):
            at = pl.ds((3 * start // 4 + i) * LANES, LANES)
            tiles.append((a_ref[:, at] + b_ref[:, at]) + (c_ref[:, at] + d_ref[:, at]))
        for i, row in enumerate(load_rows(tiles, 0)):
            out_ref[:, start + i, :] = row[:, :WIDTH]


def copies_kernel(in_ref, out_ref):
    piece = in_ref[0]
    for i in range(1, in_ref.shape[0]):
        piece = piece + in_ref[i]
    for i in range(out_ref.shape[0]):
        out_ref[i] = piece


def place_kernel(factor, layer_ref, whole_ref, out_ref):
    chans = out_ref.shape[1]
    layer = layer_ref[0]
    for b in range(3):
        rows = []
        for v in range(4):
            j = lax.rem(layer + 5 - v, 4)
            rows.append(
                jnp.concatenate(
                    [whole_ref[2 * j + h, b * chans : (b + 1) * chans] for h in range(2)], axis=1
                )
            )
        for a in range(3):
            pieces = []
            for m in range(3):
                at = (3 * a + m) * chans
                pieces += [rows[v][:, at : at + chans] for v in range(4)]
            out_ref[3 * a + b] = jnp.concatenate(pieces, axis=1) * factor


def call(kernel, outs, ins, scalars=0, scratch=()):
    return pl.pallas_call(
        kernel,
        out_shape=outs,
        in_specs=[SMEM] * scalars + [VMEM] * (ins - scalars),
        out_specs=jax.tree.map(lambda _: VMEM, outs),
        scratch_shapes=list(scratch),
        compiler_params=pltpu.CompilerParams(vmem_limit_bytes=40 << 20),
    )


def per_device(field, grad_out, filters):
    across, along = group_lists()
    spaces = lax.axis_size("space")
    chans = lax.axis_size("chan")
    chan_dev, width, rows = field.shape
    factor = 1.0 / math.sqrt(rows * width * spaces)
    layer = lax.axis_index("chan")
    kind, wide = field.dtype, jnp.float32

    def shape(*dims, dtype=kind):
        return jax.ShapeDtypeStruct(dims, dtype)

    def move(cells, step):
        return lax.ppermute(cells, "chan", [(i, (i + step) % chans) for i in range(chans)])

    def exchange(parts, groups):
        return lax.all_to_all(parts, "space", 0, 0, axis_index_groups=groups, tiled=True)

    def added(parts, copies):
        return call(copies_kernel, shape(copies, *parts.shape[1:], dtype=wide), 1)(parts)

    def by_row(cells):
        return cells.transpose(0, 2, 1)

    cells = rows * width
    code = (2 * layer + lax.axis_index("space") % NCORE)[None]
    dense = call(pack_kernel, shape(chan_dev, cells), 1)(by_row(grad_out))
    source = call(pack_kernel, shape(chan_dev, cells), 1)(by_row(field))

    def apart(cells, even, odd):
        pairs = [
            (s * chans + c, s * chans + (c + (odd if s % NCORE else even)) % chans)
            for s in range(spaces)
            for c in range(chans)
        ]
        return lax.ppermute(cells, ("space", "chan"), pairs)

    grads = [apart(dense, 4, -4), dense, apart(dense, -4, 4)]
    sources = [move(source, -2), apart(source, -1, 1), apart(source, 1, -1), source]
    edges = call(edges_kernel, shape(3 * chan_dev, LANES), 4, 1)(code, *grads)
    inner = lax.ppermute(edges, "space", [(i, i ^ 1) for i in range(spaces)])
    across_chips = [(i, i - 1) for i in range(2, spaces, 2)]
    across_chips += [(i, i + 1) for i in range(1, spaces - 1, 2)]
    outer = lax.ppermute(edges, "space", across_chips)

    own = pl.pallas_call(
        filters_kernel,
        out_shape=shape(3, 4 * chan_dev, 9 * chan_dev),
        grid_spec=pltpu.PrefetchScalarGridSpec(
            num_scalar_prefetch=1,
            grid=(1,),
            in_specs=[
                pl.BlockSpec((9, chan_dev, 12 * chan_dev), lambda i, at, j=j: (0, window_block(j, at[0]), 0))
                for j in range(4)
            ],
            out_specs=pl.BlockSpec((3, 4 * chan_dev, 9 * chan_dev), lambda i, at: (0, 0, 0)),
        ),
    )(code, filters, filters, filters, filters)

    shifted, window, ends = call(
        build_kernel,
        (
            shape(9 * chan_dev, (rows + 4) * LANES),
            shape(4 * chan_dev, rows * LANES),
            shape(4 * chan_dev, LANES),
        ),
        8,
        1,
    )(code, *grads, *sources)
    parts, borders = call(
        weights_kernel,
        (shape(8, 3 * chan_dev, LANES, dtype=wide), shape(3, 9 * chan_dev, LANES)),
        6,
        1,
    )(code, shifted, window, ends, inner, outer)
    blocks = call(inputs_kernel, (shape(chan_dev, cells, dtype=wide),) * 4, 4, 1)(
        code, shifted, own, borders
    )

    piece = added(exchange(parts, across), 1)
    piece, *blocks = lax.optimization_barrier((piece, *blocks))
    home = [
        (s * chans + c, s * chans + (c - 1 + s // (NY * NCORE)) % chans)
        for s in range(spaces)
        for c in range(chans)
    ]
    piece = lax.ppermute(piece, ("space", "chan"), home)
    others = [apart(blocks[3], 2, -2), apart(blocks[0], -1, 1), apart(blocks[2], 1, -1)]
    piece = added(exchange(added(piece, 8), along), 8)
    whole = exchange(piece, across)
    grad_filters = call(
        functools.partial(place_kernel, factor),
        shape(9, chan_dev, 12 * chan_dev, dtype=wide),
        2,
        1,
    )(layer[None], whole)
    total = call(total_kernel, shape(chan_dev, rows, width, dtype=wide), 4)(blocks[1], *others)
    return (total.transpose(0, 2, 1), grad_filters)


def solution(mesh):
    in_specs = (P("chan", "space", None), P("chan", "space", None), P())
    out_specs = (P("chan", "space", None), P(None, "chan", None))
    return jax.shard_map(
        per_device, mesh=mesh, in_specs=in_specs, out_specs=out_specs, check_vma=False
    )
```
